256 devices in a mesh: row: 16 (over x, y_lo, core), span: 2 (over y_hi), pitch: 8 (over z).
Axes of the slice: x: 4, y: 4 (y_hi: 2, y_lo: 2; y = y_hi * 2 + y_lo), z: 8, core: 2. Of those that a mesh axis runs over, the one named last changes fastest.
Arguments:
- adjoint_start: float32 [5, 64, 64, 1024], P(None, 'row', 'span', 'pitch'), may hold values from -8 to 8
- source: float32 [5, 64, 64, 1024], P(None, 'row', 'span', 'pitch'), may hold values from -6 to 6
- couplings: float32 [6, 64, 64, 1024], P(None, 'row', 'span', 'pitch'), may hold values from 0.2 to 1
- damping: float32 [64, 64, 1024], P('row', 'span', 'pitch'), may hold values from 0.1 to 0.8
- jacobians: float32 [16, 6, 5, 5], P('row')
- giles_real: float32 [15, 64, 5, 5], replicated, may hold values from -6 to 6
- giles_imag: float32 [15, 64, 5, 5], replicated, may hold values from -6 to 6
- blades: int32 [16], replicated, may hold values from 16 to 79
- mode_orders: int32 [15, 64, 2], replicated, may hold values from -2 to 2
- cell_map: int32 [16, 1024], P('row'), may hold values from 0 to 1023
Outputs:
- adjoint: float32 [5, 64, 64, 1024], P(None, 'row', 'span', 'pitch')
The draws below stay inside these ranges and needn't reach their ends.
All inputs are finite; a program needn't handle non-finite values.
Results may differ from the reference program's by a relative error of at most 0.0001.
Values sent between devices are 32-bit elements; how exact they have to be, the bound alone decides.
A program may use at most 64 MiB of HBM per device.

```python
import math
import jax
import jax.numpy as jnp
from jax import lax

CA = 4
K = 64
ITERS = 5
ROWS = 16
NA = 64
NS = 64
NP = 1024


def draw_jacobians(key, part):
    key_diagonal, key_rest = jax.random.split(key)
    diagonal = jax.random.uniform(key_diagonal, (ROWS, 6, 5, 1), jnp.float32, 0.6, 0.8)
    off_diagonal = jax.random.uniform(key_rest, (ROWS, 6, 5, 5), jnp.float32, -0.05, 0.05)
    identity = jnp.eye(5, dtype=jnp.float32)
    return off_diagonal * (1.0 - identity) + diagonal * identity


def touch_ends(drawn, own_key, least, high):
    shape = drawn.shape
    index_at = [jax.random.randint(jax.random.fold_in(own_key, axis), (), 0, shape[axis]) for axis in range(len(shape))]
    drawn = drawn.at[tuple(index_at)].set(least)
    longest = shape.index(max(shape))
    index_at[longest] = (index_at[longest] + 1) % shape[longest]
    return drawn.at[tuple(index_at)].set(high)


def block_levels(stream_key, extent, shards, low, top_value):
    def one(axis_at, shards_of):
        draws = jax.random.uniform(jax.random.fold_in(jax.random.fold_in(stream_key, 6), axis_at), (shards_of,), jnp.float32, low / len(shards), top_value / len(shards))
        return jnp.repeat(jnp.exp(draws), extent[axis_at] // shards_of).reshape((-1,) + (1,) * (len(extent) - axis_at - 1))

    loudness = one(*shards[0])
    for cut in shards[1:]:
        loudness = loudness * one(*cut)
    return loudness


def gaussian(rng, dims, spread, most, pieces=(), held_as=jnp.bfloat16):
    result = spread * jax.random.normal(rng, dims, jnp.float32)
    if pieces:
        result = result * block_levels(rng, dims, pieces, -0.22, 0.18)
    return jnp.clip(result, -most, most).astype(held_as)


def setup_inputs(seed: int = 0) -> dict:
    arg_keys = jax.random.split(jax.random.key(seed), 11)
    adjoint_start = gaussian(arg_keys[0], (5, NA, NS, NP), 2.0, 8.0, ((1, 16), (2, 2), (3, 8)), jnp.float32)
    source = gaussian(arg_keys[1], (5, NA, NS, NP), 1.0, 6.0, ((1, 16), (2, 2), (3, 8)), jnp.float32)
    couplings = jnp.clip(0.2 + 0.8 * jax.random.uniform(arg_keys[2], (6, NA, NS, NP), jnp.float32) ** block_levels(arg_keys[2], (6, NA, NS, NP), ((1, 16), (2, 2), (3, 8)), -0.2, 0.2), 0.2, 1.0)
    damping = jnp.clip(jnp.exp(math.log(0.8) - 2.0794415 * jax.random.uniform(arg_keys[3], (NA, NS, NP), jnp.float32) ** block_levels(arg_keys[3], (NA, NS, NP), ((0, 16), (1, 2), (2, 8)), -0.2, 0.2)), 0.1, 0.8)
    jacobians = draw_jacobians(jax.random.fold_in(arg_keys[10], 71), 0)
    giles_real = gaussian(arg_keys[5], (ROWS - 1, K, 5, 5), 1.0, 6.0, (), jnp.float32)
    giles_imag = gaussian(arg_keys[6], (ROWS - 1, K, 5, 5), 1.0, 6.0, (), jnp.float32)
    blades = touch_ends(jax.random.randint(arg_keys[7], (ROWS,), 16, 80), jax.random.fold_in(arg_keys[7], 1), 16, 79).astype(jnp.int32)
    mode_orders = touch_ends(jax.random.randint(arg_keys[8], (ROWS - 1, K, 2), -2, 3), jax.random.fold_in(arg_keys[8], 1), -2, 2).astype(jnp.int32)
    cell_map = touch_ends(jax.random.randint(arg_keys[9], (ROWS, NP), 0, NP), jax.random.fold_in(arg_keys[9], 1), 0, NP - 1).astype(jnp.int32)
    return {"adjoint_start": adjoint_start, "source": source, "couplings": couplings, "damping": damping, "jacobians": jacobians, "giles_real": giles_real, "giles_imag": giles_imag, "blades": blades, "mode_orders": mode_orders, "cell_map": cell_map}


PRECISE = lax.Precision.HIGHEST


def phase_table(numbers, positions, length):
    products = positions[..., :, None] * numbers[..., None, :]
    return jnp.mod(products, length).astype(jnp.float32) * (2.0 * math.pi / length)


def row_sweep(inputs):
    adjoint_row, source_row, coupling_row, diag_row, jacobian_row, boundary_row = inputs
    axial_zero = jnp.zeros_like(adjoint_row[:, :1])
    axial_next = jnp.concatenate([adjoint_row[:, 1:], axial_zero], 1)
    axial_prev = jnp.concatenate([axial_zero, adjoint_row[:, :-1]], 1)
    span_zero = jnp.zeros_like(adjoint_row[:, :, :1])
    span_next = jnp.concatenate([adjoint_row[:, :, 1:], span_zero], 2)
    span_prev = jnp.concatenate([span_zero, adjoint_row[:, :, :-1]], 2)
    pitch_next = jnp.roll(adjoint_row, -1, 3)
    pitch_prev = jnp.roll(adjoint_row, 1, 3)
    neighbours = jnp.stack([axial_next, axial_prev, span_next, span_prev, pitch_next, pitch_prev], 0)
    mixed_terms = jnp.einsum('dji,djasp->diasp', jacobian_row, neighbours, precision=PRECISE)
    coupled = jnp.sum(coupling_row[:, None] * mixed_terms, axis=0)
    right_side = source_row.at[:, CA - 1].add(boundary_row)
    return (right_side + coupled) / diag_row[None]


def to_rows(array):
    return jnp.swapaxes(array.reshape(array.shape[0], ROWS, CA, NS, NP), 0, 1)


def reference(adjoint_start, source, couplings, damping, jacobians, giles_real, giles_imag, blades, mode_orders, cell_map):
    adjoint = to_rows(adjoint_start)
    source_rows = to_rows(source)
    coupling_rows = to_rows(couplings)
    diag_sum = (damping + jnp.sum(couplings, 0)).reshape(ROWS, CA, NS, NP)
    mode_numbers = mode_orders[:, :, 0] * blades[:-1, None] + mode_orders[:, :, 1] * blades[1:, None]
    positions = jnp.broadcast_to(jnp.arange(NP, dtype=jnp.int32), (ROWS - 1, NP))
    forward_angles = phase_table(mode_numbers, positions, NP)
    forward_cos = jnp.cos(forward_angles) * (2.0 / NP)
    forward_sin = -jnp.sin(forward_angles) * (2.0 / NP)
    synth_angles = phase_table(mode_numbers, cell_map[:ROWS - 1], NP)
    synth_cos = jnp.cos(synth_angles)
    synth_sin = jnp.sin(synth_angles)
    for sweep in range(ITERS):
        strips = adjoint[1:, :, 0]
        real_part = jnp.einsum('icsp,ipk->icsk', strips, forward_cos, precision=PRECISE)
        imag_part = jnp.einsum('icsp,ipk->icsk', strips, forward_sin, precision=PRECISE)
        out_real = jnp.einsum('ikjc,ijsk->icsk', giles_real, real_part, precision=PRECISE) - jnp.einsum('ikjc,ijsk->icsk', giles_imag, imag_part, precision=PRECISE)
        out_imag = jnp.einsum('ikjc,ijsk->icsk', giles_real, imag_part, precision=PRECISE) + jnp.einsum('ikjc,ijsk->icsk', giles_imag, real_part, precision=PRECISE)
        boundary = jnp.einsum('icsk,ipk->icsp', out_real, synth_cos, precision=PRECISE) - jnp.einsum('icsk,ipk->icsp', out_imag, synth_sin, precision=PRECISE)
        boundary = jnp.concatenate([boundary, jnp.zeros((1, 5, NS, NP), jnp.float32)], 0)
        adjoint = lax.map(row_sweep, (adjoint, source_rows, coupling_rows, diag_sum, jacobians, boundary))
    return jnp.swapaxes(adjoint, 0, 1).reshape(5, NA, NS, NP)
```

```python
import math

import jax
import jax.numpy as jnp
from jax import lax
from jax.experimental import pallas as pl
from jax.experimental.pallas import tpu as pltpu
from jax.sharding import PartitionSpec as P

ITERS = 5
MESH = pl.DeviceIdType.MESH
F32 = jnp.float32
BF16 = jnp.bfloat16
I32 = jnp.int32

ROUNDS = (
    (0, (0, 1, 2, 3)),
    (1, (0, 1, 2)),
    (2, (0, 1)),
    (3, (0,)),
    (1, (3,)),
    (2, (2, 3)),
    (3, (1, 2, 3)),
    (4, (0, 1, 2, 3)),
)
ROUND_OF = {(sweep, layer): i for i, (sweep, layers) in enumerate(ROUNDS) for layer in layers}


def sine(turns, length):
    half, quarter = length // 2, length // 4
    t = ((turns + half) & (length - 1)) - half
    t = jnp.where(t > quarter, half - t, jnp.where(t < -quarter, -half - t, t))
    x = t.astype(F32) * (2.0 * math.pi / length)
    y = x * x
    poly = 1.0 / 6227020800.0
    for c in (-1.0 / 39916800.0, 1.0 / 362880.0, -1.0 / 5040.0, 1.0 / 120.0, -1.0 / 6.0):
        poly = poly * y + c
    return x + x * (y * poly)


def split(x):
    high = x.astype(BF16)
    return high, (x - high.astype(F32)).astype(BF16)


def dot(a, b):
    return jnp.dot(a, b, preferred_element_type=F32)


def lane_modes(index, blades_low, blades_high):
    comp = (index * 41) >> 10
    u = index - 25 * comp
    mode = jnp.where(u >= 12, u, 24 - u)
    first = (mode * 13) >> 6
    second = mode - 5 * first
    return comp, u, mode, (first - 2) * blades_low + (second - 2) * blades_high


def kernel(
    rows,
    pitches,
    adj_hbm,
    src_hbm,
    cpl_hbm,
    dmp_hbm,
    jac,
    gr_hbm,
    gi_hbm,
    blades,
    ord_hbm,
    map_hbm,
    out_hbm,
    buf,
    src,
    cpl,
    dmp,
    gre,
    gim,
    orders,
    donors,
    gmix,
    fwd_hi,
    fwd_lo,
    syn_hi,
    syn_lo,
    coef_out,
    coef_in,
    right_out,
    left_out,
    from_left,
    from_right,
    edge_out,
    edge_in,
    load_sem,
    store_sem,
    coef_send,
    coef_recv,
    halo_send,
    halo_recv,
):
    row, span, pitch = lax.axis_index("row"), lax.axis_index("span"), lax.axis_index("pitch")
    length = 128 * pitches
    last = rows - 1
    right, left = lax.rem(pitch + 1, pitches), lax.rem(pitch + pitches - 1, pitches)
    face = jnp.minimum(row, rows - 2)
    sent_face = jnp.maximum(row - 1, 0)

    barrier = pltpu.get_barrier_semaphore()

    def greet(target):
        pl.semaphore_signal(barrier, inc=1, device_id=target, device_id_type=MESH)

    offsets = sorted(range(pitches), key=lambda o: -min(o, pitches - o))

    @pl.when(row > 0)
    def _():
        for o in offsets:
            greet({"row": row - 1, "pitch": lax.rem(pitch + o, pitches)})

    @pl.when(row < last)
    def _():
        for o in offsets:
            greet({"row": row + 1, "pitch": lax.rem(pitch + o, pitches)})

    greet({"span": 1 - span})
    greet({"pitch": right})
    greet({"pitch": left})

    loads = [
        pltpu.make_async_copy(adj_hbm, buf.at[0], load_sem.at[0]),
        pltpu.make_async_copy(cpl_hbm, cpl, load_sem.at[1]),
        pltpu.make_async_copy(dmp_hbm, dmp, load_sem.at[2]),
        pltpu.make_async_copy(src_hbm, src, load_sem.at[3]),
        pltpu.make_async_copy(ord_hbm.at[face], orders, load_sem.at[4]),
        pltpu.make_async_copy(
            map_hbm.at[:, pl.ds(pl.multiple_of(pitch * 128, 128), 128)], donors, load_sem.at[5]
        ),
        pltpu.make_async_copy(gr_hbm, gre, load_sem.at[6]),
        pltpu.make_async_copy(gi_hbm, gim, load_sem.at[7]),
    ]
    for copy in loads:
        copy.start()

    lane = lax.broadcasted_iota(I32, (32, 128), 1)
    srow = lax.broadcasted_iota(I32, (32, 128), 0)
    block = (lane * 41) >> 10

    wide_lane = lax.broadcasted_iota(I32, (128, 128), 1)
    wide_row = lax.broadcasted_iota(I32, (128, 128), 0)
    comp, u, mode, number = lane_modes(wide_lane, blades[sent_face], blades[sent_face + 1])
    turns = number * (wide_row + pitch * 128) + jnp.where(u >= 12, length // 4, length // 2)
    table = jnp.where(comp < 5, sine(turns, length) * (2.0 / length), 0.0)
    high, low = split(table)
    fwd_hi[...] = high
    fwd_lo[...] = low

    @pl.when(row == last)
    def _():
        coef_in[...] = jnp.zeros_like(coef_in)

    def coef_copy(n, target):
        return pltpu.make_async_remote_copy(
            src_ref=coef_out.at[n],
            dst_ref=coef_in.at[n, pitch],
            send_sem=coef_send.at[n, target],
            recv_sem=coef_recv.at[n, pitch],
            device_id={"row": jnp.maximum(row - 1, 0), "pitch": target},
            device_id_type=MESH,
        )

    def coef_arrival(n, sender):
        return pltpu.make_async_copy(coef_in.at[n, sender], coef_in.at[n, sender], coef_recv.at[n, sender])

    def project(n):
        strip = buf[n, :, 0].reshape(160, 128)
        high, low = split(strip)
        both = dot(high, fwd_hi[...]) + (dot(low, fwd_hi[...]) + dot(high, fwd_lo[...]))
        total = jnp.zeros((32, 128), F32)
        for c in range(5):
            total = total + jnp.where(block == c, both[32 * c : 32 * c + 32], 0.0)
        coef_out[n] = total

    def send_coefs(n):
        @pl.when(row > 0)
        def _():
            for o in offsets:
                coef_copy(n, lax.rem(pitch + o, pitches)).start()

    def halo_copies(i):
        return (
            pltpu.make_async_remote_copy(
                src_ref=right_out.at[i],
                dst_ref=from_left.at[i],
                send_sem=halo_send.at[i, 0],
                recv_sem=halo_recv.at[i, 0],
                device_id={"pitch": right},
                device_id_type=MESH,
            ),
            pltpu.make_async_remote_copy(
                src_ref=left_out.at[i],
                dst_ref=from_right.at[i],
                send_sem=halo_send.at[i, 1],
                recv_sem=halo_recv.at[i, 1],
                device_id={"pitch": left},
                device_id_type=MESH,
            ),
            pltpu.make_async_remote_copy(
                src_ref=edge_out.at[i],
                dst_ref=edge_in.at[i],
                send_sem=halo_send.at[i, 2],
                recv_sem=halo_recv.at[i, 2],
                device_id={"span": 1 - span},
                device_id_type=MESH,
            ),
        )

    def pack(i):
        n, layers = ROUNDS[i]
        to_right = jnp.zeros((32, 128), F32)
        to_left = jnp.zeros((32, 128), F32)
        for a in layers:
            for c in range(5):
                x = buf[n, c, a]
                at = 8 * a + c
                to_right = jnp.where(lane == at, pltpu.roll(x, at + 1, 1), to_right)
                to_left = jnp.where(lane == at, pltpu.roll(x, at, 1) if at else x, to_left)
                edge_out[i, at : at + 1, :] = jnp.where(span == 0, x[31:32], x[0:1])
        right_out[i] = to_right
        left_out[i] = to_left

    def send_halo(i):
        for copy in halo_copies(i):
            copy.start()

    def wait_halo(i):
        for copy in halo_copies(i):
            copy.wait_recv()

    def sweep_layer(n, a):
        i = ROUND_OF[n, a]
        total = [src[c, a] for c in range(5)]

        def add(direction, neighbours):
            weight = cpl[direction, a]
            for c in range(5):
                mixed = jac[0, c, 0, direction] * neighbours[0]
                for j in range(1, 5):
                    mixed = mixed + jac[j, c, 0, direction] * neighbours[j]
                total[c] = total[c] + weight * mixed

        if a < 3:
            add(0, [buf[n, j, a + 1] for j in range(5)])
        if a > 0:
            add(1, [buf[n, j, a - 1] for j in range(5)])
        cells = [buf[n, j, a] for j in range(5)]
        edges = [edge_in[i, 8 * a + j : 8 * a + j + 1, :] for j in range(5)]
        add(2, [jnp.where(srow == 31, edges[j], pltpu.roll(cells[j], 31, 0)) for j in range(5)])
        add(3, [jnp.where(srow == 0, edges[j], pltpu.roll(cells[j], 1, 0)) for j in range(5)])
        ends = [from_right[i, :, 8 * a + j : 8 * a + j + 1] for j in range(5)]
        add(4, [jnp.where(lane == 127, ends[j], pltpu.roll(cells[j], 127, 1)) for j in range(5)])
        ends = [from_left[i, :, 8 * a + j : 8 * a + j + 1] for j in range(5)]
        add(5, [jnp.where(lane == 0, ends[j], pltpu.roll(cells[j], 1, 1)) for j in range(5)])
        for c in range(5):
            buf[n + 1, c, a] = total[c]

    def add_boundary(n):
        @pl.when(row < last)
        def _():
            for o in range(pitches):
                coef_arrival(n, o).wait()

        coefs = coef_in[n, 0]
        for o in range(1, pitches):
            coefs = coefs + coef_in[n, o]
        high, low = split(coefs)
        field = dot(high, syn_hi[...]) + (dot(low, syn_hi[...]) + dot(high, syn_lo[...]))
        for c in range(5):
            buf[n + 1, c, 3] = buf[n + 1, c, 3] + field[:, 128 * c : 128 * c + 128] * dmp[3]

    loads[0].wait()
    project(0)
    pack(0)

    partners = 3 + pitches * ((row > 0).astype(I32) + (row < last).astype(I32))
    pl.semaphore_wait(barrier, partners)
    send_coefs(0)
    send_halo(0)

    for copy in loads[1:4]:
        copy.wait()
    keep_next = jnp.where((srow == 31) & (span == 1), 0.0, 1.0)
    keep_prev = jnp.where((srow == 0) & (span == 0), 0.0, 1.0)
    for a in range(4):
        diag = dmp[a]
        for d in range(6):
            diag = diag + cpl[d, a]
        inverse = 1.0 / diag
        dmp[a] = inverse
        for d in range(6):
            weight = cpl[d, a] * inverse
            if d == 2:
                weight = weight * keep_next
            if d == 3:
                weight = weight * keep_prev
            cpl[d, a] = weight
        for c in range(5):
            src[c, a] = src[c, a] * inverse

    for copy in loads[4:]:
        copy.wait()
    for j in range(5):
        for c in range(5):
            gmix[5 * j + c : 5 * j + c + 1, 0:64] = gre[j, c, pl.ds(face, 1), :]
            gmix[5 * j + c : 5 * j + c + 1, 64:128] = gim[j, c, pl.ds(face, 1), :]
    gmix[25:32, :] = jnp.zeros((7, 128), F32)
    one = (orders[0:1, :] + 2) * 5 + (orders[1:2, :] + 2)
    mode_of = jnp.concatenate([one, one], axis=1)
    comp, u, mode, number = lane_modes(wide_row, blades[face], blades[face + 1])
    same = jnp.where(mode_of == mode, 1.0, 0.0)
    opposite = jnp.where(mode_of == 24 - mode, 1.0, 0.0)
    either = jnp.maximum(same, opposite)
    signed = same - opposite
    in_real = wide_lane < 64
    cosine_row = u >= 12
    for_cos = jnp.where(
        cosine_row, jnp.where(in_real, either, 0.0), jnp.where(in_real, 0.0, -signed)
    )
    for_sin = jnp.where(
        cosine_row, jnp.where(in_real, 0.0, -signed), jnp.where(in_real, -either, 0.0)
    )
    contract = (((1,), (1,)), ((), ()))
    cos_mix = lax.dot_general(
        for_cos, gmix[...], contract, precision=lax.Precision.HIGHEST, preferred_element_type=F32
    )
    sin_mix = lax.dot_general(
        for_sin, gmix[...], contract, precision=lax.Precision.HIGHEST, preferred_element_type=F32
    )
    turns = number * donors[...]
    cosine = jnp.where(comp < 5, sine(turns + length // 4, length), 0.0)
    minus = jnp.where(comp < 5, sine(turns, length), 0.0)
    pick = lax.broadcasted_iota(I32, (128, 32), 1)
    pick_comp = (lax.broadcasted_iota(I32, (128, 32), 0) * 41) >> 10
    for c in range(5):
        chosen = pick == 5 * pick_comp + c
        on_cos = jnp.sum(jnp.where(chosen, cos_mix, 0.0), axis=1, keepdims=True)
        on_sin = jnp.sum(jnp.where(chosen, sin_mix, 0.0), axis=1, keepdims=True)
        high, low = split(on_cos * cosine + on_sin * minus)
        syn_hi[:, 128 * c : 128 * c + 128] = high
        syn_lo[:, 128 * c : 128 * c + 128] = low

    wait_halo(0)
    for a in (0, 1, 2):
        sweep_layer(0, a)
    pack(1)
    send_halo(1)
    project(1)
    send_coefs(1)
    sweep_layer(0, 3)
    wait_halo(1)
    sweep_layer(1, 0)
    sweep_layer(1, 1)
    pack(2)
    send_halo(2)
    project(2)
    send_coefs(2)
    wait_halo(2)
    sweep_layer(2, 0)
    pack(3)
    send_halo(3)
    project(3)
    send_coefs(3)

    add_boundary(0)
    pack(4)
    send_halo(4)
    sweep_layer(1, 2)
    sweep_layer(2, 1)
    wait_halo(3)
    sweep_layer(3, 0)
    project(4)
    send_coefs(4)

    wait_halo(4)
    sweep_layer(1, 3)
    add_boundary(1)
    pack(5)
    send_halo(5)
    wait_halo(5)
    sweep_layer(2, 2)
    sweep_layer(2, 3)
    add_boundary(2)
    pack(6)
    send_halo(6)
    wait_halo(6)
    for a in (1, 2, 3):
        sweep_layer(3, a)
    add_boundary(3)
    pack(7)
    send_halo(7)
    wait_halo(7)
    stores = []
    for a in range(4):
        sweep_layer(4, a)
        if a == 3:
            add_boundary(4)
        copy = pltpu.make_async_copy(buf.at[5, :, a], out_hbm.at[:, a], store_sem.at[a])
        copy.start()
        stores.append(copy)

    for i in range(len(ROUNDS)):
        for copy in halo_copies(i):
            copy.wait_send()

    @pl.when(row > 0)
    def _():
        for n in range(ITERS):
            for o in range(pitches):
                coef_copy(n, o).wait_send()

    for copy in stores:
        copy.wait()


def on_device(
    rows,
    pitches,
    adjoint_start,
    source,
    couplings,
    damping,
    jacobians,
    giles_real,
    giles_imag,
    blades,
    mode_orders,
    cell_map,
):
    faces = rows - 1
    rounds = len(ROUNDS)
    anywhere = pl.BlockSpec(memory_space=pl.ANY)
    scalars = pl.BlockSpec(memory_space=pltpu.SMEM)
    dma = pltpu.SemaphoreType.DMA
    scratch = [
        pltpu.VMEM((ITERS + 1, 5, 4, 32, 128), F32),
        pltpu.VMEM((5, 4, 32, 128), F32),
        pltpu.VMEM((6, 4, 32, 128), F32),
        pltpu.VMEM((4, 32, 128), F32),
        pltpu.VMEM((5, 5, faces, 64), F32),
        pltpu.VMEM((5, 5, faces, 64), F32),
        pltpu.VMEM((2, 64), I32),
        pltpu.VMEM((1, 128), I32),
        pltpu.VMEM((32, 128), F32),
        pltpu.VMEM((128, 128), BF16),
        pltpu.VMEM((128, 128), BF16),
        pltpu.VMEM((128, 640), BF16),
        pltpu.VMEM((128, 640), BF16),
        pltpu.VMEM((ITERS, 32, 128), F32),
        pltpu.VMEM((ITERS, pitches, 32, 128), F32),
        pltpu.VMEM((rounds, 32, 128), F32),
        pltpu.VMEM((rounds, 32, 128), F32),
        pltpu.VMEM((rounds, 32, 128), F32),
        pltpu.VMEM((rounds, 32, 128), F32),
        pltpu.VMEM((rounds, 32, 128), F32),
        pltpu.VMEM((rounds, 32, 128), F32),
        dma((8,)),
        dma((4,)),
        dma((ITERS, pitches)),
        dma((ITERS, pitches)),
        dma((rounds, 3)),
        dma((rounds, 3)),
    ]

    def body(*refs):
        kernel(rows, pitches, *refs)

    return pl.pallas_call(
        body,
        name="sweeps",
        out_shape=jax.ShapeDtypeStruct(adjoint_start.shape, F32),
        in_specs=[
            anywhere,
            anywhere,
            anywhere,
            anywhere,
            scalars,
            anywhere,
            anywhere,
            scalars,
            anywhere,
            anywhere,
        ],
        out_specs=anywhere,
        scratch_shapes=scratch,
        compiler_params=pltpu.CompilerParams(collective_id=0, has_side_effects=True),
    )(
        adjoint_start,
        source,
        couplings,
        damping,
        jnp.transpose(jacobians, (2, 3, 0, 1)),
        jnp.transpose(giles_real, (2, 3, 0, 1)),
        jnp.transpose(giles_imag, (2, 3, 0, 1)),
        blades,
        jnp.transpose(mode_orders, (0, 2, 1)),
        cell_map,
    )


def solution(mesh):
    rows, pitches = mesh.shape["row"], mesh.shape["pitch"]

    def step(*args):
        return on_device(rows, pitches, *args)

    placed = (
        P(None, "row", "span", "pitch"),
        P(None, "row", "span", "pitch"),
        P(None, "row", "span", "pitch"),
        P("row", "span", "pitch"),
        P("row", None, None, None),
        P(),
        P(),
        P(),
        P(),
        P("row", None),
    )
    return jax.shard_map(
        step,
        mesh=mesh,
        in_specs=placed,
        out_specs=P(None, "row", "span", "pitch"),
        check_vma=False,
    )
```

```python
import math

import jax
import jax.numpy as jnp
from jax import lax
from jax.experimental import pallas as pl
from jax.experimental.pallas import tpu as pltpu
from jax.sharding import PartitionSpec as P

ITERS = 5
MESH = pl.DeviceIdType.MESH
F32 = jnp.float32
BF16 = jnp.bfloat16
I32 = jnp.int32

def sine(turns, length):
    half, quarter = length // 2, length // 4
    t = ((turns + half) & (length - 1)) - half
    t = jnp.where(t > quarter, half - t, jnp.where(t < -quarter, -half - t, t))
    x = t.astype(F32) * (2.0 * math.pi / length)
    y = x * x
    poly = 1.0 / 6227020800.0
    for c in (-1.0 / 39916800.0, 1.0 / 362880.0, -1.0 / 5040.0, 1.0 / 120.0, -1.0 / 6.0):
        poly = poly * y + c
    return x + x * (y * poly)


def split(x):
    high = x.astype(BF16)
    return high, (x - high.astype(F32)).astype(BF16)


def dot(a, b):
    return jnp.dot(a, b, preferred_element_type=F32)


def lane_modes(index, blades_low, blades_high):
    comp = (index * 41) >> 10
    u = index - 25 * comp
    mode = jnp.where(u >= 12, u, 24 - u)
    first = (mode * 13) >> 6
    second = mode - 5 * first
    return comp, u, mode, (first - 2) * blades_low + (second - 2) * blades_high


def kernel(
    rows,
    pitches,
    adj_hbm,
    src_hbm,
    cpl_hbm,
    dmp_hbm,
    jac,
    gr_hbm,
    gi_hbm,
    blades,
    ord_hbm,
    map_hbm,
    out_hbm,
    buf,
    src,
    cpl,
    inv,
    src_raw,
    cpl_raw,
    dmp_raw,
    result,
    gre,
    gim,
    orders,
    donors,
    gmix,
    fwd_hi,
    fwd_lo,
    syn_hi,
    syn_lo,
    coef_out,
    coef_in,
    right_out,
    left_out,
    from_left,
    from_right,
    load_sem,
    store_sem,
    coef_send,
    coef_recv,
    halo_send,
    halo_recv,
):
    row, span, pitch = lax.axis_index("row"), lax.axis_index("span"), lax.axis_index("pitch")
    length = 128 * pitches
    last = rows - 1
    right, left = lax.rem(pitch + 1, pitches), lax.rem(pitch + pitches - 1, pitches)
    face = jnp.minimum(row, rows - 2)
    upstream = jnp.maximum(row - 1, 0)
    other = 1 - span
    edge = pl.ds(pl.multiple_of(24 * other, 8), 8)

    barrier = pltpu.get_barrier_semaphore()

    def greet(target):
        pl.semaphore_signal(barrier, inc=1, device_id=target, device_id_type=MESH)

    offsets = sorted(range(pitches), key=lambda o: -min(o, pitches - o))

    def partners_of(there):
        for o in offsets:
            for half in (span, other):
                greet({"row": there, "span": half, "pitch": lax.rem(pitch + o, pitches)})

    @pl.when(row > 0)
    def _():
        partners_of(row - 1)

    @pl.when(row < last)
    def _():
        partners_of(row + 1)

    greet({"span": other})
    for side in (right, left):
        greet({"pitch": side})
        greet({"span": other, "pitch": side})

    def donor_load(slot, where):
        cells = pl.ds(pl.multiple_of(where * 128, 128), 128)
        return pltpu.make_async_copy(map_hbm.at[:, cells], donors.at[slot], load_sem.at[7 + slot])

    loads = [
        pltpu.make_async_copy(adj_hbm, buf.at[0, 0, :, :, 0:32, :], load_sem.at[0]),
        pltpu.make_async_copy(cpl_hbm, cpl_raw, load_sem.at[1]),
        pltpu.make_async_copy(dmp_hbm, dmp_raw, load_sem.at[2]),
        pltpu.make_async_copy(src_hbm, src_raw, load_sem.at[3]),
        pltpu.make_async_copy(ord_hbm.at[face], orders, load_sem.at[4]),
        pltpu.make_async_copy(gr_hbm, gre, load_sem.at[5]),
        pltpu.make_async_copy(gi_hbm, gim, load_sem.at[6]),
        donor_load(0, pitch),
        donor_load(1, right),
        donor_load(2, left),
    ]
    for copy in loads:
        copy.start()

    lane = lax.broadcasted_iota(I32, (32, 128), 1)
    long_lane = lax.broadcasted_iota(I32, (40, 128), 1)
    srow = lax.broadcasted_iota(I32, (32, 128), 0)
    block = (lane * 41) >> 10

    wide_lane = lax.broadcasted_iota(I32, (128, 128), 1)
    wide_row = lax.broadcasted_iota(I32, (128, 128), 0)
    comp, u, mode, number = lane_modes(wide_lane, blades[upstream], blades[upstream + 1])
    turns = number * (wide_row + pitch * 128) + jnp.where(u >= 12, length // 4, length // 2)
    table = jnp.where(comp < 5, sine(turns, length) * (2.0 / length), 0.0)
    high, low = split(table)
    fwd_hi[...] = high
    fwd_lo[...] = low

    @pl.when(row == last)
    def _():
        coef_in[...] = jnp.zeros_like(coef_in)

    def coef_copy(n, part, target):
        source = coef_out.at[n, edge] if part else coef_out.at[n]
        landing = pl.ds(32, 8) if part else pl.ds(0, 32)
        return pltpu.make_async_remote_copy(
            src_ref=source,
            dst_ref=coef_in.at[n, pitch, landing],
            send_sem=coef_send.at[n, part, target],
            recv_sem=coef_recv.at[n, part, pitch],
            device_id={"row": upstream, "span": other if part else span, "pitch": target},
            device_id_type=MESH,
        )

    def coef_arrival(n, part, sender):
        landing = pl.ds(32, 8) if part else pl.ds(0, 32)
        there = coef_in.at[n, sender, landing]
        return pltpu.make_async_copy(there, there, coef_recv.at[n, part, sender])

    def parts_of(n):
        return (0, 1) if n < ITERS - 1 else (0,)

    def project(n):
        strip = buf[n, 0, :, 0, 0:32, :].reshape(160, 128)
        high, low = split(strip)
        both = dot(high, fwd_hi[...]) + (dot(low, fwd_hi[...]) + dot(high, fwd_lo[...]))
        total = jnp.zeros((32, 128), F32)
        for c in range(5):
            total = total + jnp.where(block == c, both[32 * c : 32 * c + 32], 0.0)
        coef_out[n] = total

    def send_coefs(n):
        @pl.when(row > 0)
        def _():
            for part in parts_of(n):
                for o in offsets:
                    coef_copy(n, part, lax.rem(pitch + o, pitches)).start()

    def wait_coefs(n):
        @pl.when(row < last)
        def _():
            for part in parts_of(n):
                for o in range(pitches):
                    coef_arrival(n, part, o).wait()

    def halo_copy(i, source, landing, target):
        return pltpu.make_async_remote_copy(
            src_ref=source,
            dst_ref=landing,
            send_sem=halo_send.at[i],
            recv_sem=halo_recv.at[i],
            device_id=target,
            device_id_type=MESH,
        )

    side_halos = [
        halo_copy(0, right_out, from_left.at[:, 0:32, :], {"pitch": right}),
        halo_copy(1, left_out, from_right.at[:, 0:32, :], {"pitch": left}),
        halo_copy(2, right_out.at[:, edge, :], from_left.at[:, 32:40, :], {"span": other, "pitch": right}),
        halo_copy(3, left_out.at[:, edge, :], from_right.at[:, 32:40, :], {"span": other, "pitch": left}),
    ]
    start_halo = halo_copy(
        4, buf.at[0, 0, :, :, edge, :], buf.at[0, 0, :, :, 32:40, :], {"span": other}
    )
    layer_halos = [
        (
            halo_copy(5 + a, cpl.at[0, :, a, edge, :], cpl.at[0, :, a, 32:40, :], {"span": other}),
            halo_copy(9 + a, src.at[0, :, a, edge, :], src.at[0, :, a, 32:40, :], {"span": other}),
        )
        for a in range(4)
    ]
    last_halo = halo_copy(13, inv.at[0, edge, :], inv.at[0, 32:40, :], {"span": other})

    slices = []
    for a in range(4):
        slices += [(buf, (0,), (c, a)) for c in range(5)]
    for a in range(4):
        slices += [(cpl, (), (d, a)) for d in range(6) if (d, a) not in ((0, 3), (1, 0))]
        slices += [(src, (), (c, a)) for c in range(5)]
    slices.append((inv, (), ()))
    firsts = (0, 20, 30, 41, 52, 63)

    def pack():
        for tile in range(4):
            to_right = jnp.zeros((32, 128), F32)
            to_left = jnp.zeros((32, 128), F32)
            for k, (ref, before, after) in enumerate(slices[16 * tile : 16 * tile + 16]):
                x = ref[before + (0,) + after + (slice(0, 32), slice(None))]
                mine = (lane >> 3) == k
                to_left = jnp.where(mine, pltpu.roll(x, 8 * k, 1) if k else x, to_left)
                shift = (8 * k + 8) % 128
                to_right = jnp.where(mine, pltpu.roll(x, shift, 1) if shift else x, to_right)
            right_out[tile] = to_right
            left_out[tile] = to_left

    def unpack(group):
        for i in range(firsts[group], firsts[group + 1]):
            ref, before, after = slices[i]
            tile, k = i // 16, i % 16
            x, y = from_right[tile], from_left[tile]
            x = pltpu.roll(x, 128 - 8 * k, 1) if k else x
            y = pltpu.roll(y, 120 - 8 * k, 1) if k < 15 else y
            ref[before + (1,) + after] = jnp.where(long_lane < 64, x, y)

    def sweep_layer(n, a, chunks):
        for tile, lo, hi in chunks:
            total = [src[tile, c, a, lo:hi] for c in range(5)]
            at = long_lane[lo:hi]

            def add(direction, neighbours):
                weight = cpl[tile, direction, a, lo:hi]
                for c in range(5):
                    mixed = jac[0, c, 0, direction] * neighbours[0]
                    for j in range(1, 5):
                        mixed = mixed + jac[j, c, 0, direction] * neighbours[j]
                    total[c] = total[c] + weight * mixed

            if a < 3:
                add(0, [buf[n, tile, j, a + 1, lo:hi] for j in range(5)])
            if a > 0:
                add(1, [buf[n, tile, j, a - 1, lo:hi] for j in range(5)])
            columns = [buf[n, tile, j, a] for j in range(5)]
            add(2, [pltpu.roll(x, 39, 0)[lo:hi] for x in columns])
            add(3, [pltpu.roll(x, 1, 0)[lo:hi] for x in columns])
            cells = [buf[n, tile, j, a, lo:hi] for j in range(5)]
            beside = [buf[n, 1 - tile, j, a, lo:hi] for j in range(5)]
            for direction, shift, end in ((4, 127, 127), (5, 1, 0)):
                add(
                    direction,
                    [
                        jnp.where(at == end, pltpu.roll(y, shift, 1), pltpu.roll(x, shift, 1))
                        for x, y in zip(cells, beside)
                    ],
                )
            for c in range(5):
                if n == ITERS - 1:
                    result[c, a] = total[c]
                else:
                    buf[n + 1, tile, c, a, lo:hi] = total[c]

    main = ((0, 0, 32),)
    rest = ((0, 32, 40), (1, 0, 40))
    full = ((0, 0, 40), (1, 0, 40))

    def coefs_of(n, lo, hi):
        coefs = coef_in[n, 0, lo:hi]
        for o in range(1, pitches):
            coefs = coefs + coef_in[n, o, lo:hi]
        return split(coefs)

    def add_boundary(n, chunks):
        for tile, lo, hi in chunks:
            high, low = coefs_of(n, lo, hi)
            table = (slice(None), slice(640 * tile, 640 * tile + 640))
            field = dot(high, syn_hi[table]) + (dot(low, syn_hi[table]) + dot(high, syn_lo[table]))
            for c in range(5):
                share = field[:, 128 * c : 128 * c + 128] * inv[tile, lo:hi]
                if n == ITERS - 1:
                    result[c, 3] = result[c, 3] + share
                else:
                    buf[n + 1, tile, c, 3, lo:hi] = buf[n + 1, tile, c, 3, lo:hi] + share

    loads[0].wait()
    project(0)

    for copy in loads[1:4]:
        copy.wait()
    keep_next = jnp.where((srow == 31) & (span == 1), 0.0, 1.0)
    keep_prev = jnp.where((srow == 0) & (span == 0), 0.0, 1.0)
    for a in range(4):
        diag = dmp_raw[a]
        for d in range(6):
            diag = diag + cpl_raw[d, a]
        inverse = 1.0 / diag
        for d in range(6):
            weight = cpl_raw[d, a] * inverse
            if d == 2:
                weight = weight * keep_next
            if d == 3:
                weight = weight * keep_prev
            cpl[0, d, a, 0:32] = weight
        for c in range(5):
            src[0, c, a, 0:32] = src_raw[c, a] * inverse
        if a == 3:
            inv[0, 0:32] = inverse
    pack()

    pl.semaphore_wait(
        barrier, 5 + 2 * pitches * ((row > 0).astype(I32) + (row < last).astype(I32))
    )
    for copy in side_halos:
        copy.start()
    start_halo.start()
    for pair in layer_halos:
        for copy in pair:
            copy.start()
    last_halo.start()
    send_coefs(0)

    for copy in loads[4:]:
        copy.wait()
    for j in range(5):
        for c in range(5):
            gmix[5 * j + c : 5 * j + c + 1, 0:64] = gre[j, c, pl.ds(face, 1), :]
            gmix[5 * j + c : 5 * j + c + 1, 64:128] = gim[j, c, pl.ds(face, 1), :]
    gmix[25:32, :] = jnp.zeros((7, 128), F32)
    one = (orders[0:1, :] + 2) * 5 + (orders[1:2, :] + 2)
    mode_of = jnp.concatenate([one, one], axis=1)
    comp, u, mode, number = lane_modes(wide_row, blades[face], blades[face + 1])
    same = jnp.where(mode_of == mode, 1.0, 0.0)
    opposite = jnp.where(mode_of == 24 - mode, 1.0, 0.0)
    either = jnp.maximum(same, opposite)
    signed = same - opposite
    in_real = wide_lane < 64
    cosine_row = u >= 12
    for_cos = jnp.where(
        cosine_row, jnp.where(in_real, either, 0.0), jnp.where(in_real, 0.0, -signed)
    )
    for_sin = jnp.where(
        cosine_row, jnp.where(in_real, 0.0, -signed), jnp.where(in_real, -either, 0.0)
    )
    contract = (((1,), (1,)), ((), ()))
    cos_mix = lax.dot_general(
        for_cos, gmix[...], contract, precision=lax.Precision.HIGHEST, preferred_element_type=F32
    )
    sin_mix = lax.dot_general(
        for_sin, gmix[...], contract, precision=lax.Precision.HIGHEST, preferred_element_type=F32
    )
    pick = lax.broadcasted_iota(I32, (128, 32), 1)
    pick_comp = (lax.broadcasted_iota(I32, (128, 32), 0) * 41) >> 10
    beside = jnp.where(lane[0:1] < 64, donors[1], donors[2])
    for tile, cells in enumerate((donors[0], beside)):
        turns = number * cells
        cosine = jnp.where(comp < 5, sine(turns + length // 4, length), 0.0)
        minus = jnp.where(comp < 5, sine(turns, length), 0.0)
        for c in range(5):
            chosen = pick == 5 * pick_comp + c
            on_cos = jnp.sum(jnp.where(chosen, cos_mix, 0.0), axis=1, keepdims=True)
            on_sin = jnp.sum(jnp.where(chosen, sin_mix, 0.0), axis=1, keepdims=True)
            high, low = split(on_cos * cosine + on_sin * minus)
            first = 640 * tile + 128 * c
            syn_hi[:, first : first + 128] = high
            syn_lo[:, first : first + 128] = low

    def wait_sides():
        for copy in side_halos:
            copy.wait_recv()

    def wait_layer(a):
        for copy in layer_halos[a]:
            copy.wait_recv()

    def wait_start():
        start_halo.wait_recv()

    wait_sides()
    unpack(0)
    unpack(1)
    wait_start()
    wait_layer(0)
    sweep_layer(0, 0, full)
    project(1)
    send_coefs(1)
    unpack(2)
    wait_layer(1)
    sweep_layer(0, 1, full)
    sweep_layer(1, 0, full)
    project(2)
    send_coefs(2)
    unpack(3)
    wait_layer(2)
    sweep_layer(0, 2, full)
    sweep_layer(1, 1, full)
    sweep_layer(2, 0, full)
    project(3)
    send_coefs(3)

    sweep_layer(0, 3, main)
    wait_coefs(0)
    add_boundary(0, main)
    sweep_layer(1, 2, main)
    sweep_layer(2, 1, main)
    sweep_layer(3, 0, main)
    project(4)
    send_coefs(4)

    unpack(4)
    wait_layer(3)
    last_halo.wait_recv()
    sweep_layer(0, 3, rest)
    add_boundary(0, rest)
    sweep_layer(1, 2, rest)
    sweep_layer(2, 1, rest)
    sweep_layer(3, 0, rest)
    sweep_layer(1, 3, full)
    wait_coefs(1)
    add_boundary(1, full)
    sweep_layer(2, 2, full)
    sweep_layer(2, 3, full)
    wait_coefs(2)
    add_boundary(2, full)
    sweep_layer(3, 1, full)
    sweep_layer(3, 2, full)
    sweep_layer(3, 3, full)
    stores = []

    def store(a):
        copy = pltpu.make_async_copy(result.at[:, a], out_hbm.at[:, a], store_sem.at[a])
        copy.start()
        stores.append(copy)

    for a in (0, 1):
        sweep_layer(4, a, main)
        store(a)
    wait_coefs(3)
    add_boundary(3, full)
    sweep_layer(4, 2, main)
    store(2)
    sweep_layer(4, 3, main)
    wait_coefs(4)
    add_boundary(4, main)
    store(3)

    for copy in side_halos + [start_halo, last_halo]:
        copy.wait_send()
    for pair in layer_halos:
        for copy in pair:
            copy.wait_send()

    @pl.when(row > 0)
    def _():
        for n in range(ITERS):
            for part in parts_of(n):
                for o in range(pitches):
                    coef_copy(n, part, o).wait_send()

    for copy in stores:
        copy.wait()


def on_device(
    rows,
    pitches,
    adjoint_start,
    source,
    couplings,
    damping,
    jacobians,
    giles_real,
    giles_imag,
    blades,
    mode_orders,
    cell_map,
):
    faces = rows - 1
    anywhere = pl.BlockSpec(memory_space=pl.ANY)
    scalars = pl.BlockSpec(memory_space=pltpu.SMEM)
    dma = pltpu.SemaphoreType.DMA
    scratch = [
        pltpu.VMEM((ITERS, 2, 5, 4, 40, 128), F32),
        pltpu.VMEM((2, 5, 4, 40, 128), F32),
        pltpu.VMEM((2, 6, 4, 40, 128), F32),
        pltpu.VMEM((2, 40, 128), F32),
        pltpu.VMEM((5, 4, 32, 128), F32),
        pltpu.VMEM((6, 4, 32, 128), F32),
        pltpu.VMEM((4, 32, 128), F32),
        pltpu.VMEM((5, 4, 32, 128), F32),
        pltpu.VMEM((5, 5, faces, 64), F32),
        pltpu.VMEM((5, 5, faces, 64), F32),
        pltpu.VMEM((2, 64), I32),
        pltpu.VMEM((3, 1, 128), I32),
        pltpu.VMEM((32, 128), F32),
        pltpu.VMEM((128, 128), BF16),
        pltpu.VMEM((128, 128), BF16),
        pltpu.VMEM((128, 1280), BF16),
        pltpu.VMEM((128, 1280), BF16),
        pltpu.VMEM((ITERS, 32, 128), F32),
        pltpu.VMEM((ITERS, pitches, 40, 128), F32),
        pltpu.VMEM((4, 32, 128), F32),
        pltpu.VMEM((4, 32, 128), F32),
        pltpu.VMEM((4, 40, 128), F32),
        pltpu.VMEM((4, 40, 128), F32),
        dma((10,)),
        dma((4,)),
        dma((ITERS, 2, pitches)),
        dma((ITERS, 2, pitches)),
        dma((14,)),
        dma((14,)),
    ]

    def body(*refs):
        kernel(rows, pitches, *refs)

    return pl.pallas_call(
        body,
        name="sweeps",
        out_shape=jax.ShapeDtypeStruct(adjoint_start.shape, F32),
        in_specs=[
            anywhere,
            anywhere,
            anywhere,
            anywhere,
            scalars,
            anywhere,
            anywhere,
            scalars,
            anywhere,
            anywhere,
        ],
        out_specs=anywhere,
        scratch_shapes=scratch,
        compiler_params=pltpu.CompilerParams(collective_id=0, has_side_effects=True),
    )(
        adjoint_start,
        source,
        couplings,
        damping,
        jnp.transpose(jacobians, (2, 3, 0, 1)),
        jnp.transpose(giles_real, (2, 3, 0, 1)),
        jnp.transpose(giles_imag, (2, 3, 0, 1)),
        blades,
        jnp.transpose(mode_orders, (0, 2, 1)),
        cell_map,
    )


def solution(mesh):
    rows, pitches = mesh.shape["row"], mesh.shape["pitch"]

    def step(*args):
        return on_device(rows, pitches, *args)

    placed = (
        P(None, "row", "span", "pitch"),
        P(None, "row", "span", "pitch"),
        P(None, "row", "span", "pitch"),
        P("row", "span", "pitch"),
        P("row", None, None, None),
        P(),
        P(),
        P(),
        P(),
        P("row", None),
    )
    return jax.shard_map(
        step,
        mesh=mesh,
        in_specs=placed,
        out_specs=P(None, "row", "span", "pitch"),
        check_vma=False,
    )
```

```python
import math

import jax
import jax.numpy as jnp
from jax import lax
from jax.experimental import pallas as pl
from jax.experimental.pallas import tpu as pltpu
from jax.sharding import PartitionSpec as P

ITERS = 5
MESH = pl.DeviceIdType.MESH
F32 = jnp.float32
BF16 = jnp.bfloat16
I32 = jnp.int32

def sine(turns, length):
    half, quarter = length // 2, length // 4
    t = ((turns + half) & (length - 1)) - half
    t = jnp.where(t > quarter, half - t, jnp.where(t < -quarter, -half - t, t))
    x = t.astype(F32) * (2.0 * math.pi / length)
    y = x * x
    poly = 1.0 / 6227020800.0
    for c in (-1.0 / 39916800.0, 1.0 / 362880.0, -1.0 / 5040.0, 1.0 / 120.0, -1.0 / 6.0):
        poly = poly * y + c
    return x + x * (y * poly)


def split(x):
    high = x.astype(BF16)
    return high, (x - high.astype(F32)).astype(BF16)


def dot(a, b):
    return jnp.dot(a, b, preferred_element_type=F32)


def lane_modes(index, blades_low, blades_high):
    comp = (index * 41) >> 10
    u = index - 25 * comp
    mode = jnp.where(u >= 12, u, 24 - u)
    first = (mode * 13) >> 6
    second = mode - 5 * first
    return comp, u, mode, (first - 2) * blades_low + (second - 2) * blades_high


def kernel(
    rows,
    pitches,
    adj_hbm,
    src_hbm,
    cpl_hbm,
    dmp_hbm,
    jac_hbm,
    gr_hbm,
    gi_hbm,
    blades_hbm,
    ord_hbm,
    map_hbm,
    result,
    jac,
    blades,
    buf,
    cpl,
    inv,
    src_raw,
    cpl_raw,
    dmp_raw,
    giles,
    orders,
    donors,
    gmix,
    fwd_hi,
    fwd_lo,
    syn_hi,
    syn_lo,
    coef_out,
    gathered,
    reduced,
    coef_in,
    last_in,
    right_out,
    left_out,
    from_left,
    from_right,
    gauge,
    load_sem,
    sent,
    gather_recv,
    spread_recv,
    last_recv,
    halo_recv,
):
    row, span, pitch = lax.axis_index("row"), lax.axis_index("span"), lax.axis_index("pitch")
    length = 128 * pitches
    last = rows - 1
    right, left = lax.rem(pitch + 1, pitches), lax.rem(pitch + pitches - 1, pitches)
    face = jnp.minimum(row, rows - 2)
    upstream = jnp.maximum(row - 1, 0)
    other = 1 - span
    edge = pl.ds(pl.multiple_of(24 * other, 8), 8)
    near = pl.ds(pl.multiple_of(28 * other, 4), 4)
    far = pl.ds(pl.multiple_of(32 + 4 * other, 4), 4)

    barrier = pltpu.get_barrier_semaphore()

    def greet(target):
        pl.semaphore_signal(barrier, inc=1, device_id=target, device_id_type=MESH)

    offsets = sorted(range(pitches), key=lambda o: -min(o, pitches - o))

    def partners_of(there):
        for o in offsets:
            for half in (span, other):
                greet({"row": there, "span": half, "pitch": lax.rem(pitch + o, pitches)})

    def donor_load(slot, where):
        cells = pl.ds(pl.multiple_of(where * 128, 128), 128)
        return pltpu.make_async_copy(map_hbm.at[:, cells], donors.at[slot], load_sem.at[6])

    loads = [
        pltpu.make_async_copy(adj_hbm, buf.at[0, 0, :, :, 0:32, :], load_sem.at[0]),
        pltpu.make_async_copy(cpl_hbm, cpl_raw, load_sem.at[1]),
        pltpu.make_async_copy(dmp_hbm, dmp_raw, load_sem.at[2]),
        pltpu.make_async_copy(src_hbm, src_raw, load_sem.at[3]),
        pltpu.make_async_copy(blades_hbm, blades, load_sem.at[7]),
        pltpu.make_async_copy(jac_hbm, jac, load_sem.at[8]),
        pltpu.make_async_copy(ord_hbm.at[face], orders, load_sem.at[4]),
    ]
    for copy in loads:
        copy.start()
    for copy in (
        pltpu.make_async_copy(gr_hbm, giles.at[0], load_sem.at[5]),
        pltpu.make_async_copy(gi_hbm, giles.at[1], load_sem.at[5]),
        donor_load(0, pitch),
        donor_load(1, right),
        donor_load(2, left),
    ):
        copy.start()

    @pl.when(row > 0)
    def _():
        partners_of(row - 1)

    @pl.when(row < last)
    def _():
        partners_of(row + 1)

    greet({"span": other})
    for o in range(1, pitches):
        greet({"pitch": lax.rem(pitch + o, pitches)})
    for side in (right, left):
        greet({"span": other, "pitch": side})

    def take(semaphore, tiles):
        there = gauge.at[0:tiles]
        pltpu.make_async_copy(there, there, semaphore).wait()

    lane = lax.broadcasted_iota(I32, (32, 128), 1)
    long_lane = lax.broadcasted_iota(I32, (40, 128), 1)
    srow = lax.broadcasted_iota(I32, (32, 128), 0)
    block = (lane * 41) >> 10

    loads[4].wait()

    wide_lane = lax.broadcasted_iota(I32, (128, 128), 1)
    wide_row = lax.broadcasted_iota(I32, (128, 128), 0)
    comp, u, mode, number = lane_modes(wide_lane, blades[upstream], blades[upstream + 1])
    turns = number * (wide_row + pitch * 128) + jnp.where(u >= 12, length // 4, length // 2)
    table = jnp.where(comp < 5, sine(turns, length) * (2.0 / length), 0.0)
    high, low = split(table)
    fwd_hi[...] = high
    fwd_lo[...] = low

    @pl.when(row == last)
    def _():
        coef_in[...] = jnp.zeros_like(coef_in)
        last_in[...] = jnp.zeros_like(last_in)

    spread = pitches // 4
    stations = lax.div(pitch, spread)
    at_edge = stations == 3 * other

    def gather_copy(n, part):
        return pltpu.make_async_remote_copy(
            src_ref=coef_out.at[n, 8 * part : 8 * part + 8],
            dst_ref=gathered.at[n, pitch],
            send_sem=sent.at[1],
            recv_sem=gather_recv.at[n],
            device_id={"pitch": part * spread + n % spread},
            device_id_type=MESH,
        )

    def adds(n):
        return (row > 0) & (lax.rem(pitch, spread) == n % spread)

    def send_coefs(n):
        for part in range(4):
            target = part * spread + n % spread

            @pl.when((row > 0) & (pitch != target))
            def _():
                gather_copy(n, part).start()

            @pl.when((row > 0) & (pitch == target))
            def _():
                gathered[n, pitch] = coef_out[n, 8 * part : 8 * part + 8]

    def spread_copy(n, beyond, target):
        slot = 4 if beyond else stations
        landing = pl.ds(pl.multiple_of(8 * slot, 8), 8)
        return pltpu.make_async_remote_copy(
            src_ref=reduced.at[n],
            dst_ref=coef_in.at[n, landing],
            send_sem=sent.at[1 + beyond],
            recv_sem=spread_recv.at[n],
            device_id={"row": upstream, "span": other if beyond else span, "pitch": target},
            device_id_type=MESH,
        )

    def reduce_coefs(n):
        @pl.when(adds(n))
        def _():
            take(gather_recv.at[n], pitches - 1)
            total = gathered[n, 0]
            for o in range(1, pitches):
                total = total + gathered[n, o]
            reduced[n] = total
            for o in offsets:
                spread_copy(n, 0, lax.rem(pitch + o, pitches)).start()

            @pl.when(at_edge)
            def _():
                for o in offsets:
                    spread_copy(n, 1, lax.rem(pitch + o, pitches)).start()

    def wait_coefs(n):
        @pl.when(row < last)
        def _():
            take(spread_recv.at[n], 5)

    def last_copy(target):
        return pltpu.make_async_remote_copy(
            src_ref=coef_out.at[ITERS - 1],
            dst_ref=last_in.at[pitch],
            send_sem=sent.at[1],
            recv_sem=last_recv.at[0],
            device_id={"row": upstream, "pitch": target},
            device_id_type=MESH,
        )

    def send_last():
        @pl.when(row > 0)
        def _():
            for o in offsets:
                last_copy(lax.rem(pitch + o, pitches)).start()

    def wait_last():
        @pl.when(row < last)
        def _():
            take(last_recv.at[0], 4 * pitches)

    def project(n):
        strip = buf[n, 0, :, 0, 0:32, :].reshape(160, 128)
        high, low = split(strip)
        both = dot(high, fwd_hi[...]) + (dot(low, fwd_hi[...]) + dot(high, fwd_lo[...]))
        total = jnp.zeros((32, 128), F32)
        for c in range(5):
            total = total + jnp.where(block == c, both[32 * c : 32 * c + 32], 0.0)
        coef_out[n] = total

    def halo_copy(i, source, landing, target):
        return pltpu.make_async_remote_copy(
            src_ref=source,
            dst_ref=landing,
            send_sem=sent.at[0],
            recv_sem=halo_recv.at[i],
            device_id=target,
            device_id_type=MESH,
        )

    def side_copies(half):
        tiles = slice(2 * half, 2 * half + 2)
        below, beyond = slice(0, 32), slice(32, 40)
        return [
            halo_copy(
                half, right_out.at[tiles], from_left.at[tiles, below], {"pitch": right}
            ),
            halo_copy(
                half, left_out.at[tiles], from_right.at[tiles, below], {"pitch": left}
            ),
            halo_copy(
                half,
                right_out.at[tiles, edge],
                from_left.at[tiles, beyond],
                {"span": other, "pitch": right},
            ),
            halo_copy(
                half,
                left_out.at[tiles, edge],
                from_right.at[tiles, beyond],
                {"span": other, "pitch": left},
            ),
        ]

    side_halos = [side_copies(half) for half in (0, 1)]
    start_halo = halo_copy(
        2, buf.at[0, 0, :, :, edge, :], buf.at[0, 0, :, :, 32:40, :], {"span": other}
    )
    layer_halos = [
        halo_copy(3 + a, cpl.at[0, :, a, near, :], cpl.at[0, :, a, far, :], {"span": other})
        for a in range(4)
    ]
    last_halo = halo_copy(7, inv.at[0, edge, :], inv.at[0, 32:40, :], {"span": other})

    slices = []
    for a in range(4):
        slices += [(buf, (0,), (c, a)) for c in range(5)]
    for a in range(4):
        slices += [(cpl, (), (d, a)) for d in range(6) if (d, a) not in ((0, 3), (1, 0))]
        slices += [(cpl, (), (6 + c, a)) for c in range(5)]
    slices.append((inv, (), ()))
    firsts = (0, 20, 30, 41, 52, 63)

    def pack():
        low_end = (lane & 15) < 8
        for tile in range(4):
            halves = []
            for first in (16 * tile, 16 * tile + 8):
                packed = jnp.zeros((32, 128), F32)
                for k, (ref, before, after) in enumerate(slices[first : first + 8]):
                    x = ref[before + (0,) + after + (slice(0, 32), slice(None))]
                    shift = (16 * k + 8) % 128
                    packed = jnp.where((lane >> 4) == k, pltpu.roll(x, shift, 1), packed)
                halves.append(packed)
            right_out[tile] = jnp.where(low_end, halves[0], pltpu.roll(halves[1], 8, 1))
            left_out[tile] = jnp.where(low_end, pltpu.roll(halves[1], 120, 1), halves[0])

    def unpack(group):
        low_end = (long_lane & 15) < 8
        joined = {}
        for i in range(firsts[group], firsts[group + 1]):
            ref, before, after = slices[i]
            tile, half, k = i // 16, (i // 8) % 2, i % 8
            if (tile, half) not in joined:
                x, y = from_left[tile], from_right[tile]
                if half:
                    x, y = pltpu.roll(x, 120, 1), pltpu.roll(y, 8, 1)
                joined[tile, half] = jnp.where(low_end, x, y)
            ref[before + (1,) + after] = pltpu.roll(joined[tile, half], 120 - 16 * k, 1)

    def sweep_layer(n, a, chunks):
        for tile, lo, hi in chunks:
            total = [cpl[tile, 6 + c, a, lo:hi] for c in range(5)]
            at = long_lane[lo:hi]

            def add(direction, neighbours):
                weight = cpl[tile, direction, a, lo:hi]
                for c in range(5):
                    mixed = jac[0, c, 0, direction] * neighbours[0]
                    for j in range(1, 5):
                        mixed = mixed + jac[j, c, 0, direction] * neighbours[j]
                    total[c] = total[c] + weight * mixed

            if a < 3:
                add(0, [buf[n, tile, j, a + 1, lo:hi] for j in range(5)])
            if a > 0:
                add(1, [buf[n, tile, j, a - 1, lo:hi] for j in range(5)])
            columns = [buf[n, tile, j, a] for j in range(5)]
            add(2, [pltpu.roll(x, 39, 0)[lo:hi] for x in columns])
            add(3, [pltpu.roll(x, 1, 0)[lo:hi] for x in columns])
            cells = [buf[n, tile, j, a, lo:hi] for j in range(5)]
            beside = [buf[n, 1 - tile, j, a, lo:hi] for j in range(5)]
            for direction, shift, end in ((4, 127, 127), (5, 1, 0)):
                add(
                    direction,
                    [
                        jnp.where(at == end, pltpu.roll(y, shift, 1), pltpu.roll(x, shift, 1))
                        for x, y in zip(cells, beside)
                    ],
                )
            for c in range(5):
                if n == ITERS - 1:
                    result[c, a] = total[c]
                else:
                    buf[n + 1, tile, c, a, lo:hi] = total[c]

    main = ((0, 0, 32),)
    full = ((0, 0, 40), (1, 0, 40))

    def coefs_of(n, lo, hi):
        if n < ITERS - 1:
            return split(coef_in[n, lo:hi])
        coefs = last_in[0, lo:hi]
        for o in range(1, pitches):
            coefs = coefs + last_in[o, lo:hi]
        return split(coefs)

    def add_boundary(n, chunks):
        for tile, lo, hi in chunks:
            high, low = coefs_of(n, lo, hi)
            table = (slice(None), slice(640 * tile, 640 * tile + 640))
            field = dot(high, syn_hi[table]) + (dot(low, syn_hi[table]) + dot(high, syn_lo[table]))
            for c in range(5):
                share = field[:, 128 * c : 128 * c + 128] * inv[tile, lo:hi]
                if n == ITERS - 1:
                    result[c, 3] = result[c, 3] + share
                else:
                    buf[n + 1, tile, c, 3, lo:hi] = buf[n + 1, tile, c, 3, lo:hi] + share

    for copy in loads[0:4]:
        copy.wait()
    keep_next = jnp.where((srow == 31) & (span == 1), 0.0, 1.0)
    keep_prev = jnp.where((srow == 0) & (span == 0), 0.0, 1.0)
    for a in range(4):
        diag = dmp_raw[a]
        for d in range(6):
            diag = diag + cpl_raw[d, a]
        inverse = 1.0 / diag
        for d in range(6):
            weight = cpl_raw[d, a] * inverse
            if d == 2:
                weight = weight * keep_next
            if d == 3:
                weight = weight * keep_prev
            cpl[0, d, a, 0:32] = weight
        for c in range(5):
            cpl[0, 6 + c, a, 0:32] = src_raw[c, a] * inverse
        if a == 3:
            inv[0, 0:32] = inverse
    pack()

    linked = (row > 0).astype(I32) + (row < last).astype(I32)
    pl.semaphore_wait(barrier, 2 + pitches + 2 * pitches * linked)
    for copy in side_halos[0]:
        copy.start()
    start_halo.start()
    layer_halos[0].start()
    for copy in side_halos[1]:
        copy.start()
    for copy in layer_halos[1:]:
        copy.start()
    last_halo.start()
    project(0)
    send_coefs(0)

    loads[5].wait()
    loads[6].wait()
    pltpu.make_async_copy(giles, giles, load_sem.at[5]).wait()
    pltpu.make_async_copy(donors, donors, load_sem.at[6]).wait()
    for j in range(5):
        for c in range(5):
            gmix[5 * j + c : 5 * j + c + 1, 0:64] = giles[0, j, c, pl.ds(face, 1), :]
            gmix[5 * j + c : 5 * j + c + 1, 64:128] = giles[1, j, c, pl.ds(face, 1), :]
    gmix[25:32, :] = jnp.zeros((7, 128), F32)
    one = (orders[0:1, :] + 2) * 5 + (orders[1:2, :] + 2)
    mode_of = jnp.concatenate([one, one], axis=1)
    comp, u, mode, number = lane_modes(wide_row, blades[face], blades[face + 1])
    same = jnp.where(mode_of == mode, 1.0, 0.0)
    opposite = jnp.where(mode_of == 24 - mode, 1.0, 0.0)
    either = jnp.maximum(same, opposite)
    signed = same - opposite
    in_real = wide_lane < 64
    cosine_row = u >= 12
    for_cos = jnp.where(
        cosine_row, jnp.where(in_real, either, 0.0), jnp.where(in_real, 0.0, -signed)
    )
    for_sin = jnp.where(
        cosine_row, jnp.where(in_real, 0.0, -signed), jnp.where(in_real, -either, 0.0)
    )
    contract = (((1,), (1,)), ((), ()))
    cos_mix = lax.dot_general(
        for_cos, gmix[...], contract, precision=lax.Precision.HIGHEST, preferred_element_type=F32
    )
    sin_mix = lax.dot_general(
        for_sin, gmix[...], contract, precision=lax.Precision.HIGHEST, preferred_element_type=F32
    )
    pick = lax.broadcasted_iota(I32, (128, 32), 1)
    pick_comp = (lax.broadcasted_iota(I32, (128, 32), 0) * 41) >> 10
    beside = jnp.where(lane[0:1] < 64, donors[1], donors[2])
    for tile, cells in enumerate((donors[0], beside)):
        turns = number * cells
        cosine = jnp.where(comp < 5, sine(turns + length // 4, length), 0.0)
        minus = jnp.where(comp < 5, sine(turns, length), 0.0)
        for c in range(5):
            chosen = pick == 5 * pick_comp + c
            on_cos = jnp.sum(jnp.where(chosen, cos_mix, 0.0), axis=1, keepdims=True)
            on_sin = jnp.sum(jnp.where(chosen, sin_mix, 0.0), axis=1, keepdims=True)
            high, low = split(on_cos * cosine + on_sin * minus)
            first = 640 * tile + 128 * c
            syn_hi[:, first : first + 128] = high
            syn_lo[:, first : first + 128] = low

    def wait_sides(half):
        take(halo_recv.at[half], 20)

    def wait_layer(a):
        layer_halos[a].wait_recv()

    def wait_scale():
        last_halo.wait_recv()

    def wait_start():
        start_halo.wait_recv()

    reduce_coefs(0)
    wait_sides(0)
    unpack(0)
    unpack(1)
    wait_start()
    wait_layer(0)
    sweep_layer(0, 0, full)
    project(1)
    send_coefs(1)
    wait_sides(1)
    unpack(2)
    wait_layer(1)
    sweep_layer(0, 1, full)
    sweep_layer(1, 0, full)
    project(2)
    send_coefs(2)
    unpack(3)
    wait_layer(2)
    sweep_layer(0, 2, full)
    sweep_layer(1, 1, full)
    sweep_layer(2, 0, full)
    project(3)
    send_coefs(3)
    reduce_coefs(1)

    unpack(4)
    wait_layer(3)
    wait_scale()
    sweep_layer(0, 3, full)
    wait_coefs(0)
    add_boundary(0, full)
    reduce_coefs(2)
    sweep_layer(1, 2, full)
    sweep_layer(2, 1, full)
    sweep_layer(3, 0, full)
    project(4)
    send_last()

    sweep_layer(1, 3, full)
    reduce_coefs(3)
    wait_coefs(1)
    add_boundary(1, full)
    sweep_layer(2, 2, full)
    sweep_layer(2, 3, full)
    sweep_layer(3, 1, full)
    sweep_layer(4, 0, main)
    wait_coefs(2)
    add_boundary(2, full)
    sweep_layer(3, 2, full)
    sweep_layer(4, 1, main)
    sweep_layer(3, 3, full)
    wait_coefs(3)
    add_boundary(3, full)
    sweep_layer(4, 2, main)
    sweep_layer(4, 3, main)
    wait_last()
    add_boundary(4, main)

    own = (ITERS - 1) // spread
    take(sent.at[0], 83)

    @pl.when(row > 0)
    def _():
        take(sent.at[1], 16 - own + own * pitches + 4 * pitches)

    @pl.when((row > 0) & at_edge)
    def _():
        take(sent.at[2], own * pitches)


def on_device(
    rows,
    pitches,
    adjoint_start,
    source,
    couplings,
    damping,
    jacobians,
    giles_real,
    giles_imag,
    blades,
    mode_orders,
    cell_map,
):
    faces = rows - 1
    anywhere = pl.BlockSpec(memory_space=pl.ANY)
    dma = pltpu.SemaphoreType.DMA
    scratch = [
        pltpu.SMEM((5, 5, 1, 6), F32),
        pltpu.SMEM((rows,), I32),
        pltpu.VMEM((ITERS, 2, 5, 4, 40, 128), F32),
        pltpu.VMEM((2, 11, 4, 40, 128), F32),
        pltpu.VMEM((2, 40, 128), F32),
        pltpu.VMEM((5, 4, 32, 128), F32),
        pltpu.VMEM((6, 4, 32, 128), F32),
        pltpu.VMEM((4, 32, 128), F32),
        pltpu.VMEM((2, 5, 5, faces, 64), F32),
        pltpu.VMEM((2, 64), I32),
        pltpu.VMEM((3, 1, 128), I32),
        pltpu.VMEM((32, 128), F32),
        pltpu.VMEM((128, 128), BF16),
        pltpu.VMEM((128, 128), BF16),
        pltpu.VMEM((128, 1280), BF16),
        pltpu.VMEM((128, 1280), BF16),
        pltpu.VMEM((ITERS, 32, 128), F32),
        pltpu.VMEM((ITERS - 1, pitches, 8, 128), F32),
        pltpu.VMEM((ITERS - 1, 8, 128), F32),
        pltpu.VMEM((ITERS - 1, 40, 128), F32),
        pltpu.VMEM((pitches, 32, 128), F32),
        pltpu.VMEM((4, 32, 128), F32),
        pltpu.VMEM((4, 32, 128), F32),
        pltpu.VMEM((4, 40, 128), F32),
        pltpu.VMEM((4, 40, 128), F32),
        pltpu.VMEM((83, 8, 128), F32),
        dma((9,)),
        dma((3,)),
        dma((ITERS - 1,)),
        dma((ITERS - 1,)),
        dma((1,)),
        dma((8,)),
    ]

    def body(*refs):
        kernel(rows, pitches, *refs)

    return pl.pallas_call(
        body,
        name="sweeps",
        out_shape=pltpu.VMEM(adjoint_start.shape, F32),
        in_specs=[anywhere] * 10,
        out_specs=pl.BlockSpec(memory_space=pltpu.VMEM),
        scratch_shapes=scratch,
        compiler_params=pltpu.CompilerParams(collective_id=0, has_side_effects=True),
    )(
        adjoint_start,
        source,
        couplings,
        damping,
        jnp.transpose(jacobians, (2, 3, 0, 1)),
        jnp.transpose(giles_real, (2, 3, 0, 1)),
        jnp.transpose(giles_imag, (2, 3, 0, 1)),
        blades,
        jnp.transpose(mode_orders, (0, 2, 1)),
        cell_map,
    )


def solution(mesh):
    rows, pitches = mesh.shape["row"], mesh.shape["pitch"]

    def step(*args):
        return on_device(rows, pitches, *args)

    placed = (
        P(None, "row", "span", "pitch"),
        P(None, "row", "span", "pitch"),
        P(None, "row", "span", "pitch"),
        P("row", "span", "pitch"),
        P("row", None, None, None),
        P(),
        P(),
        P(),
        P(),
        P("row", None),
    )
    return jax.shard_map(
        step,
        mesh=mesh,
        in_specs=placed,
        out_specs=P(None, "row", "span", "pitch"),
        check_vma=False,
    )
```

```python
import math

import jax
import jax.numpy as jnp
from jax import lax
from jax.experimental import pallas as pl
from jax.experimental.pallas import tpu as pltpu
from jax.sharding import PartitionSpec as P

ITERS = 5
MESH = pl.DeviceIdType.MESH
F32 = jnp.float32
BF16 = jnp.bfloat16
I32 = jnp.int32

def sine(turns, length):
    half, quarter = length // 2, length // 4
    t = ((turns + half) & (length - 1)) - half
    t = jnp.where(t > quarter, half - t, jnp.where(t < -quarter, -half - t, t))
    x = t.astype(F32) * (2.0 * math.pi / length)
    y = x * x
    poly = 1.0 / 6227020800.0
    for c in (-1.0 / 39916800.0, 1.0 / 362880.0, -1.0 / 5040.0, 1.0 / 120.0, -1.0 / 6.0):
        poly = poly * y + c
    return x + x * (y * poly)


def split(x):
    high = x.astype(BF16)
    return high, (x - high.astype(F32)).astype(BF16)


def dot(a, b):
    return jnp.dot(a, b, preferred_element_type=F32)


def lane_modes(index, blades_low, blades_high):
    comp = (index * 41) >> 10
    u = index - 25 * comp
    mode = jnp.where(u >= 12, u, 24 - u)
    first = (mode * 13) >> 6
    second = mode - 5 * first
    return comp, u, mode, (first - 2) * blades_low + (second - 2) * blades_high


def kernel(
    rows,
    pitches,
    adj_hbm,
    src_hbm,
    cpl_hbm,
    dmp_hbm,
    jac_hbm,
    gr_hbm,
    gi_hbm,
    blades_hbm,
    ord_hbm,
    map_hbm,
    result,
    jac,
    blades,
    buf,
    cpl,
    inv,
    src_raw,
    cpl_raw,
    dmp_raw,
    giles,
    orders,
    donors,
    gmix,
    fwd_hi,
    fwd_lo,
    syn_hi,
    syn_lo,
    coef_out,
    gathered,
    reduced,
    coef_in,
    last_in,
    right_out,
    left_out,
    from_left,
    from_right,
    gauge,
    load_sem,
    sent,
    gather_recv,
    spread_recv,
    last_recv,
    halo_recv,
    present,
):
    row, span, pitch = lax.axis_index("row"), lax.axis_index("span"), lax.axis_index("pitch")
    length = 128 * pitches
    last = rows - 1
    right, left = lax.rem(pitch + 1, pitches), lax.rem(pitch + pitches - 1, pitches)
    face = jnp.minimum(row, rows - 2)
    upstream = jnp.maximum(row - 1, 0)
    other = 1 - span
    edge = pl.ds(pl.multiple_of(24 * other, 8), 8)
    near = pl.ds(pl.multiple_of(28 * other, 4), 4)
    far = pl.ds(pl.multiple_of(32 + 4 * other, 4), 4)

    barrier = pltpu.get_barrier_semaphore()

    def greet(target):
        pl.semaphore_signal(barrier, inc=1, device_id=target, device_id_type=MESH)

    offsets = sorted(range(pitches), key=lambda o: -min(o, pitches - o))

    def donor_load(slot, where):
        cells = pl.ds(pl.multiple_of(where * 128, 128), 128)
        return pltpu.make_async_copy(map_hbm.at[:, cells], donors.at[slot], load_sem.at[6])

    loads = [
        pltpu.make_async_copy(adj_hbm, buf.at[0, 0, :, :, 0:32, :], load_sem.at[0]),
        pltpu.make_async_copy(cpl_hbm, cpl_raw, load_sem.at[1]),
        pltpu.make_async_copy(dmp_hbm, dmp_raw, load_sem.at[2]),
        pltpu.make_async_copy(src_hbm, src_raw, load_sem.at[3]),
        pltpu.make_async_copy(blades_hbm, blades, load_sem.at[7]),
        pltpu.make_async_copy(jac_hbm, jac, load_sem.at[8]),
        pltpu.make_async_copy(ord_hbm.at[face], orders, load_sem.at[4]),
    ]
    for copy in loads:
        copy.start()
    for copy in (
        pltpu.make_async_copy(gr_hbm, giles.at[0], load_sem.at[5]),
        pltpu.make_async_copy(gi_hbm, giles.at[1], load_sem.at[5]),
        donor_load(0, pitch),
        donor_load(1, right),
        donor_load(2, left),
    ):
        copy.start()

    for there, exists in ((row - 1, row > 0), (row + 1, row < last)):

        @pl.when(exists)
        def _():
            greet({"row": there})
            greet({"row": there, "span": other})

    greet({"span": other})
    for side in (right, left):
        greet({"pitch": side})
        greet({"span": other, "pitch": side})

    def tell(semaphore, target):
        pl.semaphore_signal(semaphore, inc=1, device_id=target, device_id_type=MESH)

    def tell_ring(i):
        step = 1 + i
        for o in (step, pitches - step):
            tell(present.at[i], {"pitch": lax.rem(pitch + o, pitches)})

    def hear_ring(i):
        pl.semaphore_wait(present.at[i], 2)

    def tell_downstream():
        @pl.when(row < last)
        def _():
            tell(present.at[2], {"row": row + 1})
            tell(present.at[2], {"row": row + 1, "span": other})

    def hear_upstream():
        @pl.when(row > 0)
        def _():
            pl.semaphore_wait(present.at[2], 2)

    def take(semaphore, tiles):
        there = gauge.at[0:tiles]
        pltpu.make_async_copy(there, there, semaphore).wait()

    lane = lax.broadcasted_iota(I32, (32, 128), 1)
    long_lane = lax.broadcasted_iota(I32, (40, 128), 1)
    srow = lax.broadcasted_iota(I32, (32, 128), 0)
    block = (lane * 41) >> 10

    loads[4].wait()

    wide_lane = lax.broadcasted_iota(I32, (128, 128), 1)
    wide_row = lax.broadcasted_iota(I32, (128, 128), 0)
    comp, u, mode, number = lane_modes(wide_lane, blades[upstream], blades[upstream + 1])
    turns = number * (wide_row + pitch * 128) + jnp.where(u >= 12, length // 4, length // 2)
    table = jnp.where(comp < 5, sine(turns, length) * (2.0 / length), 0.0)
    high, low = split(table)
    fwd_hi[...] = high
    fwd_lo[...] = low

    @pl.when(row == last)
    def _():
        coef_in[...] = jnp.zeros_like(coef_in)
        last_in[...] = jnp.zeros_like(last_in)

    spread = pitches // 4
    stations = lax.div(pitch, spread)
    at_edge = stations == 3 * other

    def gather_copy(n, part):
        return pltpu.make_async_remote_copy(
            src_ref=coef_out.at[n, 8 * part : 8 * part + 8],
            dst_ref=gathered.at[n, pitch],
            send_sem=sent.at[1],
            recv_sem=gather_recv.at[n],
            device_id={"pitch": part * spread + n % spread},
            device_id_type=MESH,
        )

    def adds(n):
        return (row > 0) & (lax.rem(pitch, spread) == n % spread)

    def send_coefs(n):
        for part in range(4):
            target = part * spread + n % spread

            @pl.when((row > 0) & (pitch != target))
            def _():
                gather_copy(n, part).start()

            @pl.when((row > 0) & (pitch == target))
            def _():
                gathered[n, pitch] = coef_out[n, 8 * part : 8 * part + 8]

    def spread_copy(n, beyond, target):
        slot = 4 if beyond else stations
        landing = pl.ds(pl.multiple_of(8 * slot, 8), 8)
        return pltpu.make_async_remote_copy(
            src_ref=reduced.at[n],
            dst_ref=coef_in.at[n, landing],
            send_sem=sent.at[1 + beyond],
            recv_sem=spread_recv.at[n, beyond],
            device_id={"row": upstream, "span": other if beyond else span, "pitch": target},
            device_id_type=MESH,
        )

    def reduce_coefs(n):
        @pl.when(adds(n))
        def _():
            take(gather_recv.at[n], pitches - 1)
            total = gathered[n, 0]
            for o in range(1, pitches):
                total = total + gathered[n, o]
            reduced[n] = total
            for o in offsets:
                spread_copy(n, 0, lax.rem(pitch + o, pitches)).start()

            @pl.when(at_edge)
            def _():
                for o in offsets:
                    spread_copy(n, 1, lax.rem(pitch + o, pitches)).start()

    def wait_coefs(n, parts=(0, 1)):
        @pl.when(row < last)
        def _():
            for beyond in parts:
                take(spread_recv.at[n, beyond], 1 if beyond else 4)

    def last_copy(target):
        return pltpu.make_async_remote_copy(
            src_ref=coef_out.at[ITERS - 1],
            dst_ref=last_in.at[pitch],
            send_sem=sent.at[1],
            recv_sem=last_recv.at[0],
            device_id={"row": upstream, "pitch": target},
            device_id_type=MESH,
        )

    def send_last():
        @pl.when(row > 0)
        def _():
            for o in offsets:
                last_copy(lax.rem(pitch + o, pitches)).start()

    def wait_last():
        @pl.when(row < last)
        def _():
            take(last_recv.at[0], 4 * pitches)

    def project(n):
        strip = buf[n, 0, :, 0, 0:32, :].reshape(160, 128)
        high, low = split(strip)
        both = dot(high, fwd_hi[...]) + (dot(low, fwd_hi[...]) + dot(high, fwd_lo[...]))
        total = jnp.zeros((32, 128), F32)
        for c in range(5):
            total = total + jnp.where(block == c, both[32 * c : 32 * c + 32], 0.0)
        coef_out[n] = total

    def halo_copy(i, source, landing, target):
        return pltpu.make_async_remote_copy(
            src_ref=source,
            dst_ref=landing,
            send_sem=sent.at[0],
            recv_sem=halo_recv.at[i],
            device_id=target,
            device_id_type=MESH,
        )

    def side_copies(half):
        tiles = slice(2 * half, 2 * half + 2)
        below, beyond = slice(0, 32), slice(32, 40)
        return [
            halo_copy(
                half, right_out.at[tiles], from_left.at[tiles, below], {"pitch": right}
            ),
            halo_copy(
                half, left_out.at[tiles], from_right.at[tiles, below], {"pitch": left}
            ),
            halo_copy(
                half,
                right_out.at[tiles, edge],
                from_left.at[tiles, beyond],
                {"span": other, "pitch": right},
            ),
            halo_copy(
                half,
                left_out.at[tiles, edge],
                from_right.at[tiles, beyond],
                {"span": other, "pitch": left},
            ),
        ]

    side_halos = [side_copies(half) for half in (0, 1)]
    start_halos = [
        halo_copy(
            2 + 6 * half,
            buf.at[0, 0, :, 2 * half : 2 * half + 2, edge, :],
            buf.at[0, 0, :, 2 * half : 2 * half + 2, 32:40, :],
            {"span": other},
        )
        for half in (0, 1)
    ]
    layer_halos = [
        halo_copy(3 + a, cpl.at[0, :, a, near, :], cpl.at[0, :, a, far, :], {"span": other})
        for a in range(4)
    ]
    last_halo = halo_copy(7, inv.at[0, edge, :], inv.at[0, 32:40, :], {"span": other})

    slices = []
    for a in range(4):
        slices += [(buf, (0,), (c, a)) for c in range(5)]
    for a in range(4):
        slices += [(cpl, (), (d, a)) for d in range(6) if (d, a) not in ((0, 3), (1, 0))]
        slices += [(cpl, (), (6 + c, a)) for c in range(5)]
    slices.append((inv, (), ()))
    firsts = (0, 20, 30, 41, 52, 63)

    def pack():
        low_end = (lane & 15) < 8
        for tile in range(4):
            halves = []
            for first in (16 * tile, 16 * tile + 8):
                packed = jnp.zeros((32, 128), F32)
                for k, (ref, before, after) in enumerate(slices[first : first + 8]):
                    x = ref[before + (0,) + after + (slice(0, 32), slice(None))]
                    shift = (16 * k + 8) % 128
                    packed = jnp.where((lane >> 4) == k, pltpu.roll(x, shift, 1), packed)
                halves.append(packed)
            right_out[tile] = jnp.where(low_end, halves[0], pltpu.roll(halves[1], 8, 1))
            left_out[tile] = jnp.where(low_end, pltpu.roll(halves[1], 120, 1), halves[0])

    def unpack(group):
        low_end = (long_lane & 15) < 8
        joined = {}
        for i in range(firsts[group], firsts[group + 1]):
            ref, before, after = slices[i]
            tile, half, k = i // 16, (i // 8) % 2, i % 8
            if (tile, half) not in joined:
                x, y = from_left[tile], from_right[tile]
                if half:
                    x, y = pltpu.roll(x, 120, 1), pltpu.roll(y, 8, 1)
                joined[tile, half] = jnp.where(low_end, x, y)
            ref[before + (1,) + after] = pltpu.roll(joined[tile, half], 120 - 16 * k, 1)

    def sweep_layer(n, a, chunks):
        for tile, lo, hi in chunks:
            total = [cpl[tile, 6 + c, a, lo:hi] for c in range(5)]
            at = long_lane[lo:hi]

            def add(direction, neighbours):
                weight = cpl[tile, direction, a, lo:hi]
                for c in range(5):
                    mixed = jac[0, c, 0, direction] * neighbours[0]
                    for j in range(1, 5):
                        mixed = mixed + jac[j, c, 0, direction] * neighbours[j]
                    total[c] = total[c] + weight * mixed

            if a < 3:
                add(0, [buf[n, tile, j, a + 1, lo:hi] for j in range(5)])
            if a > 0:
                add(1, [buf[n, tile, j, a - 1, lo:hi] for j in range(5)])
            columns = [buf[n, tile, j, a] for j in range(5)]
            add(2, [pltpu.roll(x, 39, 0)[lo:hi] for x in columns])
            add(3, [pltpu.roll(x, 1, 0)[lo:hi] for x in columns])
            cells = [buf[n, tile, j, a, lo:hi] for j in range(5)]
            beside = [buf[n, 1 - tile, j, a, lo:hi] for j in range(5)]
            for direction, shift, end in ((4, 127, 127), (5, 1, 0)):
                add(
                    direction,
                    [
                        jnp.where(at == end, pltpu.roll(y, shift, 1), pltpu.roll(x, shift, 1))
                        for x, y in zip(cells, beside)
                    ],
                )
            for c in range(5):
                if n == ITERS - 1:
                    result[c, a] = total[c]
                else:
                    buf[n + 1, tile, c, a, lo:hi] = total[c]

    main = ((0, 0, 32),)
    full = ((0, 0, 40), (1, 0, 40))
    rest = ((0, 32, 40), (1, 0, 40))

    def coefs_of(n, lo, hi):
        if n < ITERS - 1:
            return split(coef_in[n, lo:hi])
        coefs = last_in[0, lo:hi]
        for o in range(1, pitches):
            coefs = coefs + last_in[o, lo:hi]
        return split(coefs)

    def add_boundary(n, chunks, ahead=False):
        for tile, lo, hi in chunks:
            high, low = coefs_of(n, lo, hi)
            table = (slice(None), slice(640 * tile, 640 * tile + 640))
            field = dot(high, syn_hi[table]) + (dot(low, syn_hi[table]) + dot(high, syn_lo[table]))
            shares = [
                field[:, 128 * c : 128 * c + 128] * inv[tile, lo:hi] for c in range(5)
            ]
            for c in range(5):
                if n == ITERS - 1:
                    result[c, 3] = result[c, 3] + shares[c]
                else:
                    buf[n + 1, tile, c, 3, lo:hi] = buf[n + 1, tile, c, 3, lo:hi] + shares[c]
            if ahead and (n < ITERS - 2 or tile == 0):
                end = hi if n < ITERS - 2 else 32
                for c in range(5):
                    mixed = jac[0, c, 0, 0] * shares[0][: end - lo]
                    for j in range(1, 5):
                        mixed = mixed + jac[j, c, 0, 0] * shares[j][: end - lo]
                    mixed = cpl[tile, 0, 2, lo:end] * mixed
                    if n < ITERS - 2:
                        buf[n + 2, tile, c, 2, lo:end] = buf[n + 2, tile, c, 2, lo:end] + mixed
                    else:
                        result[c, 2] = result[c, 2] + mixed

    for copy in loads[0:4]:
        copy.wait()
    keep_next = jnp.where((srow == 31) & (span == 1), 0.0, 1.0)
    keep_prev = jnp.where((srow == 0) & (span == 0), 0.0, 1.0)
    for a in range(4):
        diag = dmp_raw[a]
        for d in range(6):
            diag = diag + cpl_raw[d, a]
        inverse = 1.0 / diag
        for d in range(6):
            weight = cpl_raw[d, a] * inverse
            if d == 2:
                weight = weight * keep_next
            if d == 3:
                weight = weight * keep_prev
            cpl[0, d, a, 0:32] = weight
        for c in range(5):
            cpl[0, 6 + c, a, 0:32] = src_raw[c, a] * inverse
        if a == 3:
            inv[0, 0:32] = inverse
    pack()

    linked = (row > 0).astype(I32) + (row < last).astype(I32)
    pl.semaphore_wait(barrier, 5 + 2 * linked)
    tell_ring(0)
    for copy in side_halos[0] + [start_halos[0], layer_halos[0], start_halos[1]]:
        copy.start()
    for copy in side_halos[1] + layer_halos[1:] + [last_halo]:
        copy.start()
    project(0)
    hear_ring(0)
    tell_ring(1)

    loads[5].wait()
    loads[6].wait()
    pltpu.make_async_copy(giles, giles, load_sem.at[5]).wait()
    pltpu.make_async_copy(donors, donors, load_sem.at[6]).wait()
    for j in range(5):
        for c in range(5):
            gmix[5 * j + c : 5 * j + c + 1, 0:64] = giles[0, j, c, pl.ds(face, 1), :]
            gmix[5 * j + c : 5 * j + c + 1, 64:128] = giles[1, j, c, pl.ds(face, 1), :]
    gmix[25:32, :] = jnp.zeros((7, 128), F32)
    one = (orders[0:1, :] + 2) * 5 + (orders[1:2, :] + 2)
    mode_of = jnp.concatenate([one, one], axis=1)
    comp, u, mode, number = lane_modes(wide_row, blades[face], blades[face + 1])
    same = jnp.where(mode_of == mode, 1.0, 0.0)
    opposite = jnp.where(mode_of == 24 - mode, 1.0, 0.0)
    either = jnp.maximum(same, opposite)
    signed = same - opposite
    in_real = wide_lane < 64
    cosine_row = u >= 12
    for_cos = jnp.where(
        cosine_row, jnp.where(in_real, either, 0.0), jnp.where(in_real, 0.0, -signed)
    )
    for_sin = jnp.where(
        cosine_row, jnp.where(in_real, 0.0, -signed), jnp.where(in_real, -either, 0.0)
    )
    contract = (((1,), (1,)), ((), ()))
    cos_mix = lax.dot_general(
        for_cos, gmix[...], contract, precision=lax.Precision.HIGHEST, preferred_element_type=F32
    )
    sin_mix = lax.dot_general(
        for_sin, gmix[...], contract, precision=lax.Precision.HIGHEST, preferred_element_type=F32
    )
    pick = lax.broadcasted_iota(I32, (128, 32), 1)
    pick_comp = (lax.broadcasted_iota(I32, (128, 32), 0) * 41) >> 10
    beside = jnp.where(lane[0:1] < 64, donors[1], donors[2])
    for tile, cells in enumerate((donors[0], beside)):
        turns = number * cells
        cosine = jnp.where(comp < 5, sine(turns + length // 4, length), 0.0)
        minus = jnp.where(comp < 5, sine(turns, length), 0.0)
        for c in range(5):
            chosen = pick == 5 * pick_comp + c
            on_cos = jnp.sum(jnp.where(chosen, cos_mix, 0.0), axis=1, keepdims=True)
            on_sin = jnp.sum(jnp.where(chosen, sin_mix, 0.0), axis=1, keepdims=True)
            high, low = split(on_cos * cosine + on_sin * minus)
            first = 640 * tile + 128 * c
            syn_hi[:, first : first + 128] = high
            syn_lo[:, first : first + 128] = low

    def wait_sides(half):
        take(halo_recv.at[half], 20)

    def wait_layer(a):
        layer_halos[a].wait_recv()

    def wait_scale():
        last_halo.wait_recv()

    def wait_start(half):
        start_halos[half].wait_recv()

    hear_ring(1)
    tell_downstream()
    send_coefs(0)
    wait_sides(0)
    unpack(0)
    unpack(1)
    wait_start(0)
    wait_layer(0)
    sweep_layer(0, 0, main)
    project(1)
    send_coefs(1)
    sweep_layer(0, 0, rest)
    hear_upstream()
    reduce_coefs(0)
    wait_sides(1)
    unpack(2)
    wait_start(1)
    wait_layer(1)
    sweep_layer(0, 1, full)
    sweep_layer(1, 0, main)
    project(2)
    send_coefs(2)
    sweep_layer(1, 0, rest)
    unpack(3)
    wait_layer(2)
    sweep_layer(0, 2, full)
    sweep_layer(1, 1, full)
    sweep_layer(2, 0, main)
    project(3)
    send_coefs(3)
    reduce_coefs(1)
    sweep_layer(2, 0, rest)

    unpack(4)
    wait_layer(3)
    wait_scale()
    sweep_layer(0, 3, full)
    reduce_coefs(2)
    wait_coefs(0, (0,))
    add_boundary(0, main)
    sweep_layer(1, 2, main)
    sweep_layer(2, 1, main)
    sweep_layer(3, 0, main)
    project(4)
    reduce_coefs(3)
    send_last()
    wait_coefs(0, (1,))
    add_boundary(0, rest)
    sweep_layer(1, 2, rest)
    sweep_layer(2, 1, rest)
    sweep_layer(3, 0, rest)

    sweep_layer(1, 3, full)
    sweep_layer(2, 2, full)
    wait_coefs(1)
    add_boundary(1, full, ahead=True)
    sweep_layer(2, 3, full)
    sweep_layer(3, 1, full)
    sweep_layer(4, 0, main)
    wait_coefs(2)
    add_boundary(2, full)
    sweep_layer(3, 2, full)
    sweep_layer(4, 1, main)
    sweep_layer(3, 3, full)
    sweep_layer(4, 2, main)
    wait_coefs(3)
    add_boundary(3, full, ahead=True)
    sweep_layer(4, 3, main)
    wait_last()
    add_boundary(4, main)

    own = (ITERS - 1) // spread
    take(sent.at[0], 83)

    @pl.when(row > 0)
    def _():
        take(sent.at[1], 16 - own + own * pitches + 4 * pitches)

    @pl.when((row > 0) & at_edge)
    def _():
        take(sent.at[2], own * pitches)


def on_device(
    rows,
    pitches,
    adjoint_start,
    source,
    couplings,
    damping,
    jacobians,
    giles_real,
    giles_imag,
    blades,
    mode_orders,
    cell_map,
):
    faces = rows - 1
    anywhere = pl.BlockSpec(memory_space=pl.ANY)
    dma = pltpu.SemaphoreType.DMA
    scratch = [
        pltpu.SMEM((5, 5, 1, 6), F32),
        pltpu.SMEM((rows,), I32),
        pltpu.VMEM((ITERS, 2, 5, 4, 40, 128), F32),
        pltpu.VMEM((2, 11, 4, 40, 128), F32),
        pltpu.VMEM((2, 40, 128), F32),
        pltpu.VMEM((5, 4, 32, 128), F32),
        pltpu.VMEM((6, 4, 32, 128), F32),
        pltpu.VMEM((4, 32, 128), F32),
        pltpu.VMEM((2, 5, 5, faces, 64), F32),
        pltpu.VMEM((2, 64), I32),
        pltpu.VMEM((3, 1, 128), I32),
        pltpu.VMEM((32, 128), F32),
        pltpu.VMEM((128, 128), BF16),
        pltpu.VMEM((128, 128), BF16),
        pltpu.VMEM((128, 1280), BF16),
        pltpu.VMEM((128, 1280), BF16),
        pltpu.VMEM((ITERS, 32, 128), F32),
        pltpu.VMEM((ITERS - 1, pitches, 8, 128), F32),
        pltpu.VMEM((ITERS - 1, 8, 128), F32),
        pltpu.VMEM((ITERS - 1, 40, 128), F32),
        pltpu.VMEM((pitches, 32, 128), F32),
        pltpu.VMEM((4, 32, 128), F32),
        pltpu.VMEM((4, 32, 128), F32),
        pltpu.VMEM((4, 40, 128), F32),
        pltpu.VMEM((4, 40, 128), F32),
        pltpu.VMEM((83, 8, 128), F32),
        dma((9,)),
        dma((3,)),
        dma((ITERS - 1,)),
        dma((ITERS - 1, 2)),
        dma((1,)),
        dma((9,)),
        pltpu.SemaphoreType.REGULAR((3,)),
    ]

    def body(*refs):
        kernel(rows, pitches, *refs)

    return pl.pallas_call(
        body,
        name="sweeps",
        out_shape=pltpu.VMEM(adjoint_start.shape, F32),
        in_specs=[anywhere] * 10,
        out_specs=pl.BlockSpec(memory_space=pltpu.VMEM),
        scratch_shapes=scratch,
        compiler_params=pltpu.CompilerParams(collective_id=0, has_side_effects=True),
    )(
        adjoint_start,
        source,
        couplings,
        damping,
        jnp.transpose(jacobians, (2, 3, 0, 1)),
        jnp.transpose(giles_real, (2, 3, 0, 1)),
        jnp.transpose(giles_imag, (2, 3, 0, 1)),
        blades,
        jnp.transpose(mode_orders, (0, 2, 1)),
        cell_map,
    )


def solution(mesh):
    rows, pitches = mesh.shape["row"], mesh.shape["pitch"]

    def step(*args):
        return on_device(rows, pitches, *args)

    placed = (
        P(None, "row", "span", "pitch"),
        P(None, "row", "span", "pitch"),
        P(None, "row", "span", "pitch"),
        P("row", "span", "pitch"),
        P("row", None, None, None),
        P(),
        P(),
        P(),
        P(),
        P("row", None),
    )
    return jax.shard_map(
        step,
        mesh=mesh,
        in_specs=placed,
        out_specs=P(None, "row", "span", "pitch"),
        check_vma=False,
    )
```

```python
import math

import jax
import jax.numpy as jnp
from jax import lax
from jax.experimental import pallas as pl
from jax.experimental.pallas import tpu as pltpu
from jax.sharding import PartitionSpec as P

ITERS = 5
MESH = pl.DeviceIdType.MESH
F32 = jnp.float32
BF16 = jnp.bfloat16
I32 = jnp.int32

def sine(turns, length):
    half, quarter = length // 2, length // 4
    t = ((turns + half) & (length - 1)) - half
    t = jnp.where(t > quarter, half - t, jnp.where(t < -quarter, -half - t, t))
    x = t.astype(F32) * (2.0 * math.pi / length)
    y = x * x
    poly = 1.0 / 6227020800.0
    for c in (-1.0 / 39916800.0, 1.0 / 362880.0, -1.0 / 5040.0, 1.0 / 120.0, -1.0 / 6.0):
        poly = poly * y + c
    return x + x * (y * poly)


def split(x):
    high = x.astype(BF16)
    return high, (x - high.astype(F32)).astype(BF16)


def dot(a, b):
    return jnp.dot(a, b, preferred_element_type=F32)


def lane_modes(index, blades_low, blades_high):
    comp = (index * 41) >> 10
    u = index - 25 * comp
    mode = jnp.where(u >= 12, u, 24 - u)
    first = (mode * 13) >> 6
    second = mode - 5 * first
    return comp, u, mode, (first - 2) * blades_low + (second - 2) * blades_high


def kernel(
    rows,
    pitches,
    adj_hbm,
    src_hbm,
    cpl_hbm,
    dmp_hbm,
    jac_hbm,
    gr_hbm,
    gi_hbm,
    blades_hbm,
    ord_hbm,
    map_hbm,
    result,
    jac,
    blades,
    buf,
    cpl,
    inv,
    src_raw,
    cpl_raw,
    dmp_raw,
    giles,
    orders,
    donors,
    gmix,
    fwd_hi,
    fwd_lo,
    syn_hi,
    syn_lo,
    coef_out,
    gathered,
    reduced,
    coef_in,
    last_in,
    right_out,
    left_out,
    from_left,
    from_right,
    gauge,
    load_sem,
    sent,
    gather_recv,
    spread_recv,
    last_recv,
    halo_recv,
    present,
):
    row, span, pitch = lax.axis_index("row"), lax.axis_index("span"), lax.axis_index("pitch")
    length = 128 * pitches
    last = rows - 1
    right, left = lax.rem(pitch + 1, pitches), lax.rem(pitch + pitches - 1, pitches)
    face = jnp.minimum(row, rows - 2)
    upstream = jnp.maximum(row - 1, 0)
    other = 1 - span
    edge = pl.ds(pl.multiple_of(24 * other, 8), 8)
    near = pl.ds(pl.multiple_of(28 * other, 4), 4)
    far = pl.ds(pl.multiple_of(32 + 4 * other, 4), 4)

    barrier = pltpu.get_barrier_semaphore()

    def greet(target):
        pl.semaphore_signal(barrier, inc=1, device_id=target, device_id_type=MESH)

    offsets = sorted(range(pitches), key=lambda o: -min(o, pitches - o))

    def donor_load(slot, where):
        cells = pl.ds(pl.multiple_of(where * 128, 128), 128)
        return pltpu.make_async_copy(map_hbm.at[:, cells], donors.at[slot], load_sem.at[6])

    loads = [
        pltpu.make_async_copy(adj_hbm, buf.at[0, 0, :, :, 0:32, :], load_sem.at[0]),
        pltpu.make_async_copy(cpl_hbm, cpl_raw, load_sem.at[1]),
        pltpu.make_async_copy(dmp_hbm, dmp_raw, load_sem.at[2]),
        pltpu.make_async_copy(src_hbm, src_raw, load_sem.at[3]),
        pltpu.make_async_copy(blades_hbm, blades, load_sem.at[7]),
        pltpu.make_async_copy(jac_hbm, jac, load_sem.at[8]),
        pltpu.make_async_copy(ord_hbm.at[face], orders, load_sem.at[4]),
    ]
    for copy in loads:
        copy.start()
    for copy in (
        pltpu.make_async_copy(gr_hbm, giles.at[0], load_sem.at[5]),
        pltpu.make_async_copy(gi_hbm, giles.at[1], load_sem.at[5]),
        donor_load(0, pitch),
        donor_load(1, right),
        donor_load(2, left),
    ):
        copy.start()

    for there, exists in ((row - 1, row > 0), (row + 1, row < last)):

        @pl.when(exists)
        def _():
            greet({"row": there})
            greet({"row": there, "span": other})

    greet({"span": other})
    for side in (right, left):
        greet({"pitch": side})
        greet({"span": other, "pitch": side})
    for o in (2, pitches - 2):
        greet({"pitch": lax.rem(pitch + o, pitches)})

    def tell(semaphore, target):
        pl.semaphore_signal(semaphore, inc=1, device_id=target, device_id_type=MESH)

    def tell_ring():
        for o in (2, pitches - 2):
            tell(present.at[0], {"pitch": lax.rem(pitch + o, pitches)})

    def hear_ring():
        pl.semaphore_wait(present.at[0], 2)

    def tell_downstream():
        @pl.when(row < last)
        def _():
            tell(present.at[1], {"row": row + 1})
            tell(present.at[1], {"row": row + 1, "span": other})

    def hear_upstream():
        @pl.when(row > 0)
        def _():
            pl.semaphore_wait(present.at[1], 2)

    def take(semaphore, tiles):
        there = gauge.at[0:tiles]
        pltpu.make_async_copy(there, there, semaphore).wait()

    lane = lax.broadcasted_iota(I32, (32, 128), 1)
    long_lane = lax.broadcasted_iota(I32, (40, 128), 1)
    srow = lax.broadcasted_iota(I32, (32, 128), 0)
    block = (lane * 41) >> 10

    loads[4].wait()

    wide_lane = lax.broadcasted_iota(I32, (128, 128), 1)
    wide_row = lax.broadcasted_iota(I32, (128, 128), 0)
    comp, u, mode, number = lane_modes(wide_lane, blades[upstream], blades[upstream + 1])
    turns = number * (wide_row + pitch * 128) + jnp.where(u >= 12, length // 4, length // 2)
    table = jnp.where(comp < 5, sine(turns, length) * (2.0 / length), 0.0)
    high, low = split(table)
    fwd_hi[...] = high
    fwd_lo[...] = low

    @pl.when(row == last)
    def _():
        coef_in[...] = jnp.zeros_like(coef_in)
        last_in[...] = jnp.zeros_like(last_in)

    spread = pitches // 4
    stations = lax.div(pitch, spread)
    at_edge = stations == 3 * other

    def gather_copy(n, part):
        return pltpu.make_async_remote_copy(
            src_ref=coef_out.at[n, 8 * part : 8 * part + 8],
            dst_ref=gathered.at[n, pitch],
            send_sem=sent.at[1],
            recv_sem=gather_recv.at[n],
            device_id={"pitch": part * spread + n % spread},
            device_id_type=MESH,
        )

    def adds(n):
        return (row > 0) & (lax.rem(pitch, spread) == n % spread)

    def send_coefs(n):
        for part in range(4):
            target = part * spread + n % spread

            @pl.when((row > 0) & (pitch != target))
            def _():
                gather_copy(n, part).start()

            @pl.when((row > 0) & (pitch == target))
            def _():
                gathered[n, pitch] = coef_out[n, 8 * part : 8 * part + 8]

    def spread_copy(n, beyond, target):
        slot = 4 if beyond else stations
        landing = pl.ds(pl.multiple_of(8 * slot, 8), 8)
        return pltpu.make_async_remote_copy(
            src_ref=reduced.at[n],
            dst_ref=coef_in.at[n, landing],
            send_sem=sent.at[1 + beyond],
            recv_sem=spread_recv.at[n, beyond],
            device_id={"row": upstream, "span": other if beyond else span, "pitch": target},
            device_id_type=MESH,
        )

    def reduce_coefs(n):
        @pl.when(adds(n))
        def _():
            take(gather_recv.at[n], pitches - 1)
            total = gathered[n, 0]
            for o in range(1, pitches):
                total = total + gathered[n, o]
            reduced[n] = total
            for o in offsets:
                spread_copy(n, 0, lax.rem(pitch + o, pitches)).start()

            @pl.when(at_edge)
            def _():
                for o in offsets:
                    spread_copy(n, 1, lax.rem(pitch + o, pitches)).start()

    def wait_coefs(n, parts=(0, 1)):
        @pl.when(row < last)
        def _():
            for beyond in parts:
                take(spread_recv.at[n, beyond], 1 if beyond else 4)

    def last_copy(target):
        return pltpu.make_async_remote_copy(
            src_ref=coef_out.at[ITERS - 1],
            dst_ref=last_in.at[pitch],
            send_sem=sent.at[1],
            recv_sem=last_recv.at[0],
            device_id={"row": upstream, "pitch": target},
            device_id_type=MESH,
        )

    def send_last():
        @pl.when(row > 0)
        def _():
            for o in offsets:
                last_copy(lax.rem(pitch + o, pitches)).start()

    def wait_last():
        @pl.when(row < last)
        def _():
            take(last_recv.at[0], 4 * pitches)

    def project(n):
        strip = buf[n, 0, :, 0, 0:32, :].reshape(160, 128)
        high, low = split(strip)
        both = dot(high, fwd_hi[...]) + (dot(low, fwd_hi[...]) + dot(high, fwd_lo[...]))
        total = jnp.zeros((32, 128), F32)
        for c in range(5):
            total = total + jnp.where(block == c, both[32 * c : 32 * c + 32], 0.0)
        coef_out[n] = total

    def halo_copy(i, source, landing, target):
        return pltpu.make_async_remote_copy(
            src_ref=source,
            dst_ref=landing,
            send_sem=sent.at[0],
            recv_sem=halo_recv.at[i],
            device_id=target,
            device_id_type=MESH,
        )

    def side_copies(half):
        tiles = slice(2 * half, 2 * half + 2)
        below, beyond = slice(0, 32), slice(32, 40)
        return [
            halo_copy(
                half, right_out.at[tiles], from_left.at[tiles, below], {"pitch": right}
            ),
            halo_copy(
                half, left_out.at[tiles], from_right.at[tiles, below], {"pitch": left}
            ),
            halo_copy(
                half,
                right_out.at[tiles, edge],
                from_left.at[tiles, beyond],
                {"span": other, "pitch": right},
            ),
            halo_copy(
                half,
                left_out.at[tiles, edge],
                from_right.at[tiles, beyond],
                {"span": other, "pitch": left},
            ),
        ]

    side_halos = [side_copies(half) for half in (0, 1)]
    start_halos = [
        halo_copy(
            2 + 6 * half,
            buf.at[0, 0, :, 2 * half : 2 * half + 2, edge, :],
            buf.at[0, 0, :, 2 * half : 2 * half + 2, 32:40, :],
            {"span": other},
        )
        for half in (0, 1)
    ]
    layer_halos = [
        halo_copy(3 + a, cpl.at[0, :, a, near, :], cpl.at[0, :, a, far, :], {"span": other})
        for a in range(4)
    ]
    last_halo = halo_copy(7, inv.at[0, edge, :], inv.at[0, 32:40, :], {"span": other})

    slices = []
    for a in range(4):
        slices += [(buf, (0,), (c, a)) for c in range(5)]
    for a in range(4):
        slices += [(cpl, (), (d, a)) for d in range(6) if (d, a) not in ((0, 3), (1, 0))]
        slices += [(cpl, (), (6 + c, a)) for c in range(5)]
    slices.append((inv, (), ()))
    firsts = (0, 20, 30, 41, 52, 63)

    def pack():
        low_end = (lane & 15) < 8
        for tile in range(4):
            halves = []
            for first in (16 * tile, 16 * tile + 8):
                packed = jnp.zeros((32, 128), F32)
                for k, (ref, before, after) in enumerate(slices[first : first + 8]):
                    x = ref[before + (0,) + after + (slice(0, 32), slice(None))]
                    shift = (16 * k + 8) % 128
                    packed = jnp.where((lane >> 4) == k, pltpu.roll(x, shift, 1), packed)
                halves.append(packed)
            right_out[tile] = jnp.where(low_end, halves[0], pltpu.roll(halves[1], 8, 1))
            left_out[tile] = jnp.where(low_end, pltpu.roll(halves[1], 120, 1), halves[0])

    def unpack(group):
        low_end = (long_lane & 15) < 8
        joined = {}
        for i in range(firsts[group], firsts[group + 1]):
            ref, before, after = slices[i]
            tile, half, k = i // 16, (i // 8) % 2, i % 8
            if (tile, half) not in joined:
                x, y = from_left[tile], from_right[tile]
                if half:
                    x, y = pltpu.roll(x, 120, 1), pltpu.roll(y, 8, 1)
                joined[tile, half] = jnp.where(low_end, x, y)
            ref[before + (1,) + after] = pltpu.roll(joined[tile, half], 120 - 16 * k, 1)

    def sweep_layer(n, a, chunks):
        for tile, lo, hi in chunks:
            total = [cpl[tile, 6 + c, a, lo:hi] for c in range(5)]
            at = long_lane[lo:hi]

            def add(direction, neighbours):
                weight = cpl[tile, direction, a, lo:hi]
                for c in range(5):
                    mixed = jac[0, c, 0, direction] * neighbours[0]
                    for j in range(1, 5):
                        mixed = mixed + jac[j, c, 0, direction] * neighbours[j]
                    total[c] = total[c] + weight * mixed

            if a < 3:
                add(0, [buf[n, tile, j, a + 1, lo:hi] for j in range(5)])
            if a > 0:
                add(1, [buf[n, tile, j, a - 1, lo:hi] for j in range(5)])
            columns = [buf[n, tile, j, a] for j in range(5)]
            add(2, [pltpu.roll(x, 39, 0)[lo:hi] for x in columns])
            add(3, [pltpu.roll(x, 1, 0)[lo:hi] for x in columns])
            cells = [buf[n, tile, j, a, lo:hi] for j in range(5)]
            beside = [buf[n, 1 - tile, j, a, lo:hi] for j in range(5)]
            for direction, shift, end in ((4, 127, 127), (5, 1, 0)):
                add(
                    direction,
                    [
                        jnp.where(at == end, pltpu.roll(y, shift, 1), pltpu.roll(x, shift, 1))
                        for x, y in zip(cells, beside)
                    ],
                )
            for c in range(5):
                if n == ITERS - 1:
                    result[c, a] = total[c]
                else:
                    buf[n + 1, tile, c, a, lo:hi] = total[c]

    main = ((0, 0, 32),)
    full = ((0, 0, 40), (1, 0, 40))
    rest = ((0, 32, 40), (1, 0, 40))

    def coefs_of(n, lo, hi):
        if n < ITERS - 1:
            return split(coef_in[n, lo:hi])
        coefs = last_in[0, lo:hi]
        for o in range(1, pitches):
            coefs = coefs + last_in[o, lo:hi]
        return split(coefs)

    def add_boundary(n, chunks, ahead=False):
        for tile, lo, hi in chunks:
            high, low = coefs_of(n, lo, hi)
            table = (slice(None), slice(640 * tile, 640 * tile + 640))
            field = dot(high, syn_hi[table]) + (dot(low, syn_hi[table]) + dot(high, syn_lo[table]))
            shares = [
                field[:, 128 * c : 128 * c + 128] * inv[tile, lo:hi] for c in range(5)
            ]
            for c in range(5):
                if n == ITERS - 1:
                    result[c, 3] = result[c, 3] + shares[c]
                else:
                    buf[n + 1, tile, c, 3, lo:hi] = buf[n + 1, tile, c, 3, lo:hi] + shares[c]
            if ahead and (n < ITERS - 2 or tile == 0):
                end = hi if n < ITERS - 2 else 32
                for c in range(5):
                    mixed = jac[0, c, 0, 0] * shares[0][: end - lo]
                    for j in range(1, 5):
                        mixed = mixed + jac[j, c, 0, 0] * shares[j][: end - lo]
                    mixed = cpl[tile, 0, 2, lo:end] * mixed
                    if n < ITERS - 2:
                        buf[n + 2, tile, c, 2, lo:end] = buf[n + 2, tile, c, 2, lo:end] + mixed
                    else:
                        result[c, 2] = result[c, 2] + mixed

    for copy in loads[0:4]:
        copy.wait()
    keep_next = jnp.where((srow == 31) & (span == 1), 0.0, 1.0)
    keep_prev = jnp.where((srow == 0) & (span == 0), 0.0, 1.0)
    for a in range(4):
        diag = dmp_raw[a]
        for d in range(6):
            diag = diag + cpl_raw[d, a]
        inverse = 1.0 / diag
        for d in range(6):
            weight = cpl_raw[d, a] * inverse
            if d == 2:
                weight = weight * keep_next
            if d == 3:
                weight = weight * keep_prev
            cpl[0, d, a, 0:32] = weight
        for c in range(5):
            cpl[0, 6 + c, a, 0:32] = src_raw[c, a] * inverse
        if a == 3:
            inv[0, 0:32] = inverse
    pack()

    linked = (row > 0).astype(I32) + (row < last).astype(I32)
    pl.semaphore_wait(barrier, 7 + 2 * linked)
    tell_ring()
    for copy in side_halos[0] + [start_halos[0], layer_halos[0], start_halos[1]]:
        copy.start()
    for copy in side_halos[1] + layer_halos[1:] + [last_halo]:
        copy.start()
    project(0)
    hear_ring()
    tell_downstream()
    send_coefs(0)

    loads[5].wait()
    loads[6].wait()
    pltpu.make_async_copy(giles, giles, load_sem.at[5]).wait()
    pltpu.make_async_copy(donors, donors, load_sem.at[6]).wait()
    for j in range(5):
        for c in range(5):
            gmix[5 * j + c : 5 * j + c + 1, 0:64] = giles[0, j, c, pl.ds(face, 1), :]
            gmix[5 * j + c : 5 * j + c + 1, 64:128] = giles[1, j, c, pl.ds(face, 1), :]
    gmix[25:32, :] = jnp.zeros((7, 128), F32)
    one = (orders[0:1, :] + 2) * 5 + (orders[1:2, :] + 2)
    mode_of = jnp.concatenate([one, one], axis=1)
    comp, u, mode, number = lane_modes(wide_row, blades[face], blades[face + 1])
    same = jnp.where(mode_of == mode, 1.0, 0.0)
    opposite = jnp.where(mode_of == 24 - mode, 1.0, 0.0)
    either = jnp.maximum(same, opposite)
    signed = same - opposite
    in_real = wide_lane < 64
    cosine_row = u >= 12
    for_cos = jnp.where(
        cosine_row, jnp.where(in_real, either, 0.0), jnp.where(in_real, 0.0, -signed)
    )
    for_sin = jnp.where(
        cosine_row, jnp.where(in_real, 0.0, -signed), jnp.where(in_real, -either, 0.0)
    )
    contract = (((1,), (1,)), ((), ()))
    cos_mix = lax.dot_general(
        for_cos, gmix[...], contract, precision=lax.Precision.HIGHEST, preferred_element_type=F32
    )
    sin_mix = lax.dot_general(
        for_sin, gmix[...], contract, precision=lax.Precision.HIGHEST, preferred_element_type=F32
    )
    pick = lax.broadcasted_iota(I32, (128, 32), 1)
    pick_comp = (lax.broadcasted_iota(I32, (128, 32), 0) * 41) >> 10
    beside = jnp.where(lane[0:1] < 64, donors[1], donors[2])
    for tile, cells in enumerate((donors[0], beside)):
        turns = number * cells
        cosine = jnp.where(comp < 5, sine(turns + length // 4, length), 0.0)
        minus = jnp.where(comp < 5, sine(turns, length), 0.0)
        for c in range(5):
            chosen = pick == 5 * pick_comp + c
            on_cos = jnp.sum(jnp.where(chosen, cos_mix, 0.0), axis=1, keepdims=True)
            on_sin = jnp.sum(jnp.where(chosen, sin_mix, 0.0), axis=1, keepdims=True)
            high, low = split(on_cos * cosine + on_sin * minus)
            first = 640 * tile + 128 * c
            syn_hi[:, first : first + 128] = high
            syn_lo[:, first : first + 128] = low

    def wait_sides(half):
        take(halo_recv.at[half], 20)

    def wait_layer(a):
        layer_halos[a].wait_recv()

    def wait_scale():
        last_halo.wait_recv()

    def wait_start(half):
        start_halos[half].wait_recv()

    wait_sides(0)
    unpack(0)
    unpack(1)
    wait_start(0)
    wait_layer(0)
    sweep_layer(0, 0, main)
    project(1)
    send_coefs(1)
    hear_upstream()
    reduce_coefs(0)
    sweep_layer(0, 0, rest)
    wait_sides(1)
    unpack(2)
    wait_start(1)
    wait_layer(1)
    sweep_layer(0, 1, full)
    sweep_layer(1, 0, main)
    project(2)
    send_coefs(2)
    sweep_layer(1, 0, rest)
    unpack(3)
    wait_layer(2)
    sweep_layer(0, 2, full)
    sweep_layer(1, 1, full)
    sweep_layer(2, 0, main)
    project(3)
    send_coefs(3)
    reduce_coefs(1)
    sweep_layer(2, 0, rest)

    unpack(4)
    wait_layer(3)
    wait_scale()
    sweep_layer(0, 3, full)
    reduce_coefs(2)
    wait_coefs(0, (0,))
    add_boundary(0, main)
    sweep_layer(1, 2, main)
    sweep_layer(2, 1, main)
    sweep_layer(3, 0, main)
    project(4)
    reduce_coefs(3)
    send_last()
    wait_coefs(0, (1,))
    add_boundary(0, rest)
    sweep_layer(1, 2, rest)
    sweep_layer(2, 1, rest)
    sweep_layer(3, 0, rest)

    sweep_layer(1, 3, full)
    sweep_layer(2, 2, full)
    wait_coefs(1)
    add_boundary(1, full, ahead=True)
    sweep_layer(2, 3, full)
    sweep_layer(3, 1, full)
    sweep_layer(4, 0, main)
    wait_coefs(2)
    add_boundary(2, full)
    sweep_layer(3, 2, full)
    sweep_layer(4, 1, main)
    sweep_layer(3, 3, full)
    sweep_layer(4, 2, main)
    wait_coefs(3)
    add_boundary(3, full, ahead=True)
    sweep_layer(4, 3, main)
    wait_last()
    add_boundary(4, main)

    own = (ITERS - 1) // spread
    take(sent.at[0], 83)

    @pl.when(row > 0)
    def _():
        take(sent.at[1], 16 - own + own * pitches + 4 * pitches)

    @pl.when((row > 0) & at_edge)
    def _():
        take(sent.at[2], own * pitches)


def on_device(
    rows,
    pitches,
    adjoint_start,
    source,
    couplings,
    damping,
    jacobians,
    giles_real,
    giles_imag,
    blades,
    mode_orders,
    cell_map,
):
    faces = rows - 1
    anywhere = pl.BlockSpec(memory_space=pl.ANY)
    dma = pltpu.SemaphoreType.DMA
    scratch = [
        pltpu.SMEM((5, 5, 1, 6), F32),
        pltpu.SMEM((rows,), I32),
        pltpu.VMEM((ITERS, 2, 5, 4, 40, 128), F32),
        pltpu.VMEM((2, 11, 4, 40, 128), F32),
        pltpu.VMEM((2, 40, 128), F32),
        pltpu.VMEM((5, 4, 32, 128), F32),
        pltpu.VMEM((6, 4, 32, 128), F32),
        pltpu.VMEM((4, 32, 128), F32),
        pltpu.VMEM((2, 5, 5, faces, 64), F32),
        pltpu.VMEM((2, 64), I32),
        pltpu.VMEM((3, 1, 128), I32),
        pltpu.VMEM((32, 128), F32),
        pltpu.VMEM((128, 128), BF16),
        pltpu.VMEM((128, 128), BF16),
        pltpu.VMEM((128, 1280), BF16),
        pltpu.VMEM((128, 1280), BF16),
        pltpu.VMEM((ITERS, 32, 128), F32),
        pltpu.VMEM((ITERS - 1, pitches, 8, 128), F32),
        pltpu.VMEM((ITERS - 1, 8, 128), F32),
        pltpu.VMEM((ITERS - 1, 40, 128), F32),
        pltpu.VMEM((pitches, 32, 128), F32),
        pltpu.VMEM((4, 32, 128), F32),
        pltpu.VMEM((4, 32, 128), F32),
        pltpu.VMEM((4, 40, 128), F32),
        pltpu.VMEM((4, 40, 128), F32),
        pltpu.VMEM((83, 8, 128), F32),
        dma((9,)),
        dma((3,)),
        dma((ITERS - 1,)),
        dma((ITERS - 1, 2)),
        dma((1,)),
        dma((9,)),
        pltpu.SemaphoreType.REGULAR((2,)),
    ]

    def body(*refs):
        kernel(rows, pitches, *refs)

    return pl.pallas_call(
        body,
        name="sweeps",
        out_shape=pltpu.VMEM(adjoint_start.shape, F32),
        in_specs=[anywhere] * 10,
        out_specs=pl.BlockSpec(memory_space=pltpu.VMEM),
        scratch_shapes=scratch,
        compiler_params=pltpu.CompilerParams(collective_id=0, has_side_effects=True),
    )(
        adjoint_start,
        source,
        couplings,
        damping,
        jnp.transpose(jacobians, (2, 3, 0, 1)),
        jnp.transpose(giles_real, (2, 3, 0, 1)),
        jnp.transpose(giles_imag, (2, 3, 0, 1)),
        blades,
        jnp.transpose(mode_orders, (0, 2, 1)),
        cell_map,
    )


def solution(mesh):
    rows, pitches = mesh.shape["row"], mesh.shape["pitch"]

    def step(*args):
        return on_device(rows, pitches, *args)

    placed = (
        P(None, "row", "span", "pitch"),
        P(None, "row", "span", "pitch"),
        P(None, "row", "span", "pitch"),
        P("row", "span", "pitch"),
        P("row", None, None, None),
        P(),
        P(),
        P(),
        P(),
        P("row", None),
    )
    return jax.shard_map(
        step,
        mesh=mesh,
        in_specs=placed,
        out_specs=P(None, "row", "span", "pitch"),
        check_vma=False,
    )
```

```python
import math

import jax
import jax.numpy as jnp
from jax import lax
from jax.experimental import pallas as pl
from jax.experimental.pallas import tpu as pltpu
from jax.sharding import PartitionSpec as P

ITERS = 5
MESH = pl.DeviceIdType.MESH
F32 = jnp.float32
BF16 = jnp.bfloat16
I32 = jnp.int32

def sine(turns, length):
    half, quarter = length // 2, length // 4
    t = ((turns + half) & (length - 1)) - half
    t = jnp.where(t > quarter, half - t, jnp.where(t < -quarter, -half - t, t))
    x = t.astype(F32) * (2.0 * math.pi / length)
    y = x * x
    poly = 1.0 / 6227020800.0
    for c in (-1.0 / 39916800.0, 1.0 / 362880.0, -1.0 / 5040.0, 1.0 / 120.0, -1.0 / 6.0):
        poly = poly * y + c
    return x + x * (y * poly)


def split(x):
    high = x.astype(BF16)
    return high, (x - high.astype(F32)).astype(BF16)


def dot(a, b):
    return jnp.dot(a, b, preferred_element_type=F32)


def lane_modes(index, blades_low, blades_high):
    comp = (index * 41) >> 10
    u = index - 25 * comp
    mode = jnp.where(u >= 12, u, 24 - u)
    first = (mode * 13) >> 6
    second = mode - 5 * first
    return comp, u, mode, (first - 2) * blades_low + (second - 2) * blades_high


def kernel(
    rows,
    pitches,
    adj_hbm,
    src_hbm,
    cpl_hbm,
    dmp_hbm,
    jac_hbm,
    gr_hbm,
    gi_hbm,
    blades_hbm,
    ord_hbm,
    map_hbm,
    result,
    jac,
    blades,
    buf,
    cpl,
    inv,
    src_raw,
    cpl_raw,
    dmp_raw,
    giles,
    orders,
    donors,
    gmix,
    fwd_hi,
    fwd_lo,
    syn_hi,
    syn_lo,
    coef_out,
    gathered,
    reduced,
    coef_in,
    last_in,
    right_out,
    left_out,
    from_left,
    from_right,
    gauge,
    load_sem,
    sent,
    gather_recv,
    spread_recv,
    last_recv,
    halo_recv,
    present,
):
    row, span, pitch = lax.axis_index("row"), lax.axis_index("span"), lax.axis_index("pitch")
    length = 128 * pitches
    last = rows - 1
    right, left = lax.rem(pitch + 1, pitches), lax.rem(pitch + pitches - 1, pitches)
    face = jnp.minimum(row, rows - 2)
    upstream = jnp.maximum(row - 1, 0)
    other = 1 - span
    edge = pl.ds(pl.multiple_of(24 * other, 8), 8)
    near = pl.ds(pl.multiple_of(28 * other, 4), 4)
    far = pl.ds(pl.multiple_of(32 + 4 * other, 4), 4)

    barrier = pltpu.get_barrier_semaphore()

    def greet(target):
        pl.semaphore_signal(barrier, inc=1, device_id=target, device_id_type=MESH)

    offsets = sorted(range(pitches), key=lambda o: -min(o, pitches - o))

    def donor_load(slot, where):
        cells = pl.ds(pl.multiple_of(where * 128, 128), 128)
        return pltpu.make_async_copy(map_hbm.at[:, cells], donors.at[slot], load_sem.at[6])

    loads = [
        pltpu.make_async_copy(adj_hbm, buf.at[0, 0, :, :, 0:32, :], load_sem.at[0]),
        pltpu.make_async_copy(cpl_hbm, cpl_raw, load_sem.at[1]),
        pltpu.make_async_copy(dmp_hbm, dmp_raw, load_sem.at[2]),
        pltpu.make_async_copy(src_hbm, src_raw, load_sem.at[3]),
        pltpu.make_async_copy(blades_hbm, blades, load_sem.at[7]),
        pltpu.make_async_copy(jac_hbm, jac, load_sem.at[8]),
        pltpu.make_async_copy(ord_hbm.at[face], orders, load_sem.at[4]),
    ]
    for copy in loads:
        copy.start()
    for copy in (
        pltpu.make_async_copy(gr_hbm, giles.at[0], load_sem.at[5]),
        pltpu.make_async_copy(gi_hbm, giles.at[1], load_sem.at[5]),
        donor_load(0, pitch),
        donor_load(1, right),
        donor_load(2, left),
    ):
        copy.start()

    for there, exists in ((row - 1, row > 0), (row + 1, row < last)):

        @pl.when(exists)
        def _():
            greet({"row": there})
            greet({"row": there, "span": other})

    greet({"span": other})
    for side in (right, left):
        greet({"pitch": side})
        greet({"span": other, "pitch": side})
    for o in (2, pitches - 2):
        greet({"pitch": lax.rem(pitch + o, pitches)})

    def tell(semaphore, target):
        pl.semaphore_signal(semaphore, inc=1, device_id=target, device_id_type=MESH)

    def tell_ring():
        for o in (2, pitches - 2):
            tell(present.at[0], {"pitch": lax.rem(pitch + o, pitches)})

    def hear_ring():
        pl.semaphore_wait(present.at[0], 2)

    def tell_downstream():
        @pl.when(row < last)
        def _():
            tell(present.at[1], {"row": row + 1})
            tell(present.at[1], {"row": row + 1, "span": other})

    def hear_upstream():
        @pl.when(row > 0)
        def _():
            pl.semaphore_wait(present.at[1], 2)

    def take(semaphore, tiles):
        there = gauge.at[0:tiles]
        pltpu.make_async_copy(there, there, semaphore).wait()

    lane = lax.broadcasted_iota(I32, (32, 128), 1)
    long_lane = lax.broadcasted_iota(I32, (40, 128), 1)
    srow = lax.broadcasted_iota(I32, (32, 128), 0)
    block = (lane * 41) >> 10

    loads[4].wait()

    wide_lane = lax.broadcasted_iota(I32, (128, 128), 1)
    wide_row = lax.broadcasted_iota(I32, (128, 128), 0)
    comp, u, mode, number = lane_modes(wide_lane, blades[upstream], blades[upstream + 1])
    turns = number * (wide_row + pitch * 128) + jnp.where(u >= 12, length // 4, length // 2)
    table = jnp.where(comp < 5, sine(turns, length) * (2.0 / length), 0.0)
    high, low = split(table)
    fwd_hi[...] = high
    fwd_lo[...] = low

    @pl.when(row == last)
    def _():
        coef_in[...] = jnp.zeros_like(coef_in)
        last_in[...] = jnp.zeros_like(last_in)

    spread = pitches // 4
    stations = lax.div(pitch, spread)
    at_edge = stations == 3 * other

    def gather_copy(n, part):
        return pltpu.make_async_remote_copy(
            src_ref=coef_out.at[n, 8 * part : 8 * part + 8],
            dst_ref=gathered.at[n, pitch],
            send_sem=sent.at[1],
            recv_sem=gather_recv.at[n],
            device_id={"pitch": part * spread + n % spread},
            device_id_type=MESH,
        )

    def adds(n):
        return (row > 0) & (lax.rem(pitch, spread) == n % spread)

    def send_coefs(n):
        for part in range(4):
            target = part * spread + n % spread

            @pl.when((row > 0) & (pitch != target))
            def _():
                gather_copy(n, part).start()

            @pl.when((row > 0) & (pitch == target))
            def _():
                gathered[n, pitch] = coef_out[n, 8 * part : 8 * part + 8]

    def spread_copy(n, beyond, target):
        slot = 4 if beyond else stations
        landing = pl.ds(pl.multiple_of(8 * slot, 8), 8)
        return pltpu.make_async_remote_copy(
            src_ref=reduced.at[n],
            dst_ref=coef_in.at[n, landing],
            send_sem=sent.at[1 + beyond],
            recv_sem=spread_recv.at[n, beyond],
            device_id={"row": upstream, "span": other if beyond else span, "pitch": target},
            device_id_type=MESH,
        )

    def reduce_coefs(n):
        @pl.when(adds(n))
        def _():
            take(gather_recv.at[n], pitches - 1)
            total = gathered[n, 0]
            for o in range(1, pitches):
                total = total + gathered[n, o]
            reduced[n] = total
            for o in offsets:
                spread_copy(n, 0, lax.rem(pitch + o, pitches)).start()

            @pl.when(at_edge)
            def _():
                for o in offsets:
                    spread_copy(n, 1, lax.rem(pitch + o, pitches)).start()

    def wait_coefs(n, parts=(0, 1)):
        @pl.when(row < last)
        def _():
            for beyond in parts:
                take(spread_recv.at[n, beyond], 1 if beyond else 4)

    def last_copy(target):
        return pltpu.make_async_remote_copy(
            src_ref=coef_out.at[ITERS - 1],
            dst_ref=last_in.at[pitch],
            send_sem=sent.at[1],
            recv_sem=last_recv.at[0],
            device_id={"row": upstream, "pitch": target},
            device_id_type=MESH,
        )

    def send_last():
        @pl.when(row > 0)
        def _():
            for o in offsets:
                last_copy(lax.rem(pitch + o, pitches)).start()

    def wait_last():
        @pl.when(row < last)
        def _():
            take(last_recv.at[0], 4 * pitches)

    def project(n):
        strip = buf[n, 0, :, 0, 0:32, :].reshape(160, 128)
        high, low = split(strip)
        both = dot(high, fwd_hi[...]) + (dot(low, fwd_hi[...]) + dot(high, fwd_lo[...]))
        total = jnp.zeros((32, 128), F32)
        for c in range(5):
            total = total + jnp.where(block == c, both[32 * c : 32 * c + 32], 0.0)
        coef_out[n] = total

    def halo_copy(i, source, landing, target):
        return pltpu.make_async_remote_copy(
            src_ref=source,
            dst_ref=landing,
            send_sem=sent.at[0],
            recv_sem=halo_recv.at[i],
            device_id=target,
            device_id_type=MESH,
        )

    def side_copies(half):
        tiles = slice(2 * half, 2 * half + 2)
        below, beyond = slice(0, 32), slice(32, 40)
        return [
            halo_copy(
                half, right_out.at[tiles], from_left.at[tiles, below], {"pitch": right}
            ),
            halo_copy(
                half, left_out.at[tiles], from_right.at[tiles, below], {"pitch": left}
            ),
            halo_copy(
                half,
                right_out.at[tiles, edge],
                from_left.at[tiles, beyond],
                {"span": other, "pitch": right},
            ),
            halo_copy(
                half,
                left_out.at[tiles, edge],
                from_right.at[tiles, beyond],
                {"span": other, "pitch": left},
            ),
        ]

    side_halos = [side_copies(half) for half in (0, 1)]
    start_halos = [
        halo_copy(
            2 + 6 * half,
            buf.at[0, 0, :, 2 * half : 2 * half + 2, edge, :],
            buf.at[0, 0, :, 2 * half : 2 * half + 2, 32:40, :],
            {"span": other},
        )
        for half in (0, 1)
    ]
    layer_halos = [
        halo_copy(3 + a, cpl.at[0, :, a, near, :], cpl.at[0, :, a, far, :], {"span": other})
        for a in range(4)
    ]
    last_halo = halo_copy(7, inv.at[0, edge, :], inv.at[0, 32:40, :], {"span": other})

    slices = []
    for a in range(4):
        slices += [(buf, (0,), (c, a)) for c in range(5)]
    for a in range(4):
        slices += [(cpl, (), (d, a)) for d in range(6) if (d, a) not in ((0, 3), (1, 0))]
        slices += [(cpl, (), (6 + c, a)) for c in range(5)]
    slices.append((inv, (), ()))
    firsts = (0, 20, 30, 41, 52, 63)

    def pack():
        low_end = (lane & 15) < 8
        for tile in range(4):
            halves = []
            for first in (16 * tile, 16 * tile + 8):
                packed = jnp.zeros((32, 128), F32)
                for k, (ref, before, after) in enumerate(slices[first : first + 8]):
                    x = ref[before + (0,) + after + (slice(0, 32), slice(None))]
                    shift = (16 * k + 8) % 128
                    packed = jnp.where((lane >> 4) == k, pltpu.roll(x, shift, 1), packed)
                halves.append(packed)
            right_out[tile] = jnp.where(low_end, halves[0], pltpu.roll(halves[1], 8, 1))
            left_out[tile] = jnp.where(low_end, pltpu.roll(halves[1], 120, 1), halves[0])

    def unpack(group):
        low_end = (long_lane & 15) < 8
        joined = {}
        for i in range(firsts[group], firsts[group + 1]):
            ref, before, after = slices[i]
            tile, half, k = i // 16, (i // 8) % 2, i % 8
            if (tile, half) not in joined:
                x, y = from_left[tile], from_right[tile]
                if half:
                    x, y = pltpu.roll(x, 120, 1), pltpu.roll(y, 8, 1)
                joined[tile, half] = jnp.where(low_end, x, y)
            ref[before + (1,) + after] = pltpu.roll(joined[tile, half], 120 - 16 * k, 1)

    def sweep_layer(n, a, chunks):
        for tile, lo, hi in chunks:
            total = [cpl[tile, 6 + c, a, lo:hi] for c in range(5)]
            at = long_lane[lo:hi]

            def add(direction, neighbours):
                weight = cpl[tile, direction, a, lo:hi]
                for c in range(5):
                    mixed = jac[0, c, 0, direction] * neighbours[0]
                    for j in range(1, 5):
                        mixed = mixed + jac[j, c, 0, direction] * neighbours[j]
                    total[c] = total[c] + weight * mixed

            if a < 3:
                add(0, [buf[n, tile, j, a + 1, lo:hi] for j in range(5)])
            if a > 0:
                add(1, [buf[n, tile, j, a - 1, lo:hi] for j in range(5)])
            columns = [buf[n, tile, j, a] for j in range(5)]
            add(2, [pltpu.roll(x, 39, 0)[lo:hi] for x in columns])
            add(3, [pltpu.roll(x, 1, 0)[lo:hi] for x in columns])
            cells = [buf[n, tile, j, a, lo:hi] for j in range(5)]
            beside = [buf[n, 1 - tile, j, a, lo:hi] for j in range(5)]
            for direction, shift, end in ((4, 127, 127), (5, 1, 0)):
                add(
                    direction,
                    [
                        jnp.where(at == end, pltpu.roll(y, shift, 1), pltpu.roll(x, shift, 1))
                        for x, y in zip(cells, beside)
                    ],
                )
            for c in range(5):
                if n == ITERS - 1:
                    result[c, a] = total[c]
                else:
                    buf[n + 1, tile, c, a, lo:hi] = total[c]

    main = ((0, 0, 32),)
    full = ((0, 0, 40), (1, 0, 40))
    rest = ((0, 32, 40), (1, 0, 40))

    def coefs_of(n, lo, hi):
        if n < ITERS - 1:
            return split(coef_in[n, lo:hi])
        coefs = last_in[0, lo:hi]
        for o in range(1, pitches):
            coefs = coefs + last_in[o, lo:hi]
        return split(coefs)

    def add_boundary(n, chunks, ahead=0):
        for tile, lo, hi in chunks:
            high, low = coefs_of(n, lo, hi)
            table = (slice(None), slice(640 * tile, 640 * tile + 640))
            field = dot(high, syn_hi[table]) + (dot(low, syn_hi[table]) + dot(high, syn_lo[table]))
            shares = [
                field[:, 128 * c : 128 * c + 128] * inv[tile, lo:hi] for c in range(5)
            ]
            for c in range(5):
                if n == ITERS - 1:
                    result[c, 3] = result[c, 3] + shares[c]
                else:
                    buf[n + 1, tile, c, 3, lo:hi] = buf[n + 1, tile, c, 3, lo:hi] + shares[c]
            if n == ITERS - 2 and tile:
                continue
            end = 32 if n == ITERS - 2 else hi
            above = [share[: end - lo] for share in shares]
            for depth in range(1, ahead + 1):
                layer, then = 3 - depth, n + 1 + depth
                passed = []
                for c in range(5):
                    mixed = jac[0, c, 0, 0] * above[0]
                    for j in range(1, 5):
                        mixed = mixed + jac[j, c, 0, 0] * above[j]
                    passed.append(cpl[tile, 0, layer, lo:end] * mixed)
                above = passed
                for c in range(5):
                    if then == ITERS:
                        result[c, layer] = result[c, layer] + above[c]
                    else:
                        old = buf[then, tile, c, layer, lo:end]
                        buf[then, tile, c, layer, lo:end] = old + above[c]

    for copy in loads[0:4]:
        copy.wait()
    keep_next = jnp.where((srow == 31) & (span == 1), 0.0, 1.0)
    keep_prev = jnp.where((srow == 0) & (span == 0), 0.0, 1.0)
    for a in range(4):
        diag = dmp_raw[a]
        for d in range(6):
            diag = diag + cpl_raw[d, a]
        inverse = 1.0 / diag
        for d in range(6):
            weight = cpl_raw[d, a] * inverse
            if d == 2:
                weight = weight * keep_next
            if d == 3:
                weight = weight * keep_prev
            cpl[0, d, a, 0:32] = weight
        for c in range(5):
            cpl[0, 6 + c, a, 0:32] = src_raw[c, a] * inverse
        if a == 3:
            inv[0, 0:32] = inverse
    pack()

    linked = (row > 0).astype(I32) + (row < last).astype(I32)
    pl.semaphore_wait(barrier, 7 + 2 * linked)
    tell_ring()
    for copy in side_halos[0] + [start_halos[0], layer_halos[0], start_halos[1]]:
        copy.start()
    for copy in side_halos[1] + layer_halos[1:] + [last_halo]:
        copy.start()
    project(0)
    hear_ring()
    tell_downstream()
    send_coefs(0)

    loads[5].wait()
    loads[6].wait()
    pltpu.make_async_copy(giles, giles, load_sem.at[5]).wait()
    pltpu.make_async_copy(donors, donors, load_sem.at[6]).wait()
    for j in range(5):
        for c in range(5):
            gmix[5 * j + c : 5 * j + c + 1, 0:64] = giles[0, j, c, pl.ds(face, 1), :]
            gmix[5 * j + c : 5 * j + c + 1, 64:128] = giles[1, j, c, pl.ds(face, 1), :]
    gmix[25:32, :] = jnp.zeros((7, 128), F32)
    one = (orders[0:1, :] + 2) * 5 + (orders[1:2, :] + 2)
    mode_of = jnp.concatenate([one, one], axis=1)
    comp, u, mode, number = lane_modes(wide_row, blades[face], blades[face + 1])
    same = jnp.where(mode_of == mode, 1.0, 0.0)
    opposite = jnp.where(mode_of == 24 - mode, 1.0, 0.0)
    either = jnp.maximum(same, opposite)
    signed = same - opposite
    in_real = wide_lane < 64
    cosine_row = u >= 12
    for_cos = jnp.where(
        cosine_row, jnp.where(in_real, either, 0.0), jnp.where(in_real, 0.0, -signed)
    )
    for_sin = jnp.where(
        cosine_row, jnp.where(in_real, 0.0, -signed), jnp.where(in_real, -either, 0.0)
    )
    contract = (((1,), (1,)), ((), ()))
    cos_mix = lax.dot_general(
        for_cos, gmix[...], contract, precision=lax.Precision.HIGHEST, preferred_element_type=F32
    )
    sin_mix = lax.dot_general(
        for_sin, gmix[...], contract, precision=lax.Precision.HIGHEST, preferred_element_type=F32
    )
    pick = lax.broadcasted_iota(I32, (128, 32), 1)
    pick_comp = (lax.broadcasted_iota(I32, (128, 32), 0) * 41) >> 10
    beside = jnp.where(lane[0:1] < 64, donors[1], donors[2])
    for tile, cells in enumerate((donors[0], beside)):
        turns = number * cells
        cosine = jnp.where(comp < 5, sine(turns + length // 4, length), 0.0)
        minus = jnp.where(comp < 5, sine(turns, length), 0.0)
        for c in range(5):
            chosen = pick == 5 * pick_comp + c
            on_cos = jnp.sum(jnp.where(chosen, cos_mix, 0.0), axis=1, keepdims=True)
            on_sin = jnp.sum(jnp.where(chosen, sin_mix, 0.0), axis=1, keepdims=True)
            high, low = split(on_cos * cosine + on_sin * minus)
            first = 640 * tile + 128 * c
            syn_hi[:, first : first + 128] = high
            syn_lo[:, first : first + 128] = low

    def wait_sides(half):
        take(halo_recv.at[half], 20)

    def wait_layer(a):
        layer_halos[a].wait_recv()

    def wait_scale():
        last_halo.wait_recv()

    def wait_start(half):
        start_halos[half].wait_recv()

    wait_sides(0)
    unpack(0)
    unpack(1)
    wait_start(0)
    wait_layer(0)
    sweep_layer(0, 0, main)
    project(1)
    send_coefs(1)
    hear_upstream()
    reduce_coefs(0)
    sweep_layer(0, 0, rest)
    wait_sides(1)
    unpack(2)
    wait_start(1)
    wait_layer(1)
    sweep_layer(0, 1, full)
    sweep_layer(1, 0, main)
    project(2)
    send_coefs(2)
    sweep_layer(1, 0, rest)
    unpack(3)
    wait_layer(2)
    sweep_layer(0, 2, full)
    sweep_layer(1, 1, full)
    sweep_layer(2, 0, main)
    project(3)
    send_coefs(3)
    reduce_coefs(1)
    sweep_layer(2, 0, rest)

    unpack(4)
    wait_layer(3)
    wait_scale()
    sweep_layer(0, 3, full)
    sweep_layer(1, 2, main)
    reduce_coefs(2)
    sweep_layer(2, 1, main)
    sweep_layer(3, 0, main)
    wait_coefs(0, (0,))
    add_boundary(0, main, ahead=3)
    project(4)
    reduce_coefs(3)
    send_last()
    wait_coefs(0, (1,))
    add_boundary(0, rest)
    sweep_layer(1, 2, rest)
    sweep_layer(2, 1, rest)
    sweep_layer(3, 0, rest)

    sweep_layer(1, 3, full)
    sweep_layer(2, 2, full)
    wait_coefs(1)
    add_boundary(1, full, ahead=1)
    sweep_layer(2, 3, full)
    sweep_layer(3, 1, full)
    sweep_layer(4, 0, main)
    wait_coefs(2)
    add_boundary(2, full)
    sweep_layer(3, 2, full)
    sweep_layer(4, 1, main)
    sweep_layer(3, 3, full)
    sweep_layer(4, 2, main)
    wait_coefs(3)
    add_boundary(3, full, ahead=1)
    sweep_layer(4, 3, main)
    wait_last()
    add_boundary(4, main)

    own = (ITERS - 1) // spread
    take(sent.at[0], 83)

    @pl.when(row > 0)
    def _():
        take(sent.at[1], 16 - own + own * pitches + 4 * pitches)

    @pl.when((row > 0) & at_edge)
    def _():
        take(sent.at[2], own * pitches)


def on_device(
    rows,
    pitches,
    adjoint_start,
    source,
    couplings,
    damping,
    jacobians,
    giles_real,
    giles_imag,
    blades,
    mode_orders,
    cell_map,
):
    faces = rows - 1
    anywhere = pl.BlockSpec(memory_space=pl.ANY)
    dma = pltpu.SemaphoreType.DMA
    scratch = [
        pltpu.SMEM((5, 5, 1, 6), F32),
        pltpu.SMEM((rows,), I32),
        pltpu.VMEM((ITERS, 2, 5, 4, 40, 128), F32),
        pltpu.VMEM((2, 11, 4, 40, 128), F32),
        pltpu.VMEM((2, 40, 128), F32),
        pltpu.VMEM((5, 4, 32, 128), F32),
        pltpu.VMEM((6, 4, 32, 128), F32),
        pltpu.VMEM((4, 32, 128), F32),
        pltpu.VMEM((2, 5, 5, faces, 64), F32),
        pltpu.VMEM((2, 64), I32),
        pltpu.VMEM((3, 1, 128), I32),
        pltpu.VMEM((32, 128), F32),
        pltpu.VMEM((128, 128), BF16),
        pltpu.VMEM((128, 128), BF16),
        pltpu.VMEM((128, 1280), BF16),
        pltpu.VMEM((128, 1280), BF16),
        pltpu.VMEM((ITERS, 32, 128), F32),
        pltpu.VMEM((ITERS - 1, pitches, 8, 128), F32),
        pltpu.VMEM((ITERS - 1, 8, 128), F32),
        pltpu.VMEM((ITERS - 1, 40, 128), F32),
        pltpu.VMEM((pitches, 32, 128), F32),
        pltpu.VMEM((4, 32, 128), F32),
        pltpu.VMEM((4, 32, 128), F32),
        pltpu.VMEM((4, 40, 128), F32),
        pltpu.VMEM((4, 40, 128), F32),
        pltpu.VMEM((83, 8, 128), F32),
        dma((9,)),
        dma((3,)),
        dma((ITERS - 1,)),
        dma((ITERS - 1, 2)),
        dma((1,)),
        dma((9,)),
        pltpu.SemaphoreType.REGULAR((2,)),
    ]

    def body(*refs):
        kernel(rows, pitches, *refs)

    return pl.pallas_call(
        body,
        name="sweeps",
        out_shape=pltpu.VMEM(adjoint_start.shape, F32),
        in_specs=[anywhere] * 10,
        out_specs=pl.BlockSpec(memory_space=pltpu.VMEM),
        scratch_shapes=scratch,
        compiler_params=pltpu.CompilerParams(collective_id=0, has_side_effects=True),
    )(
        adjoint_start,
        source,
        couplings,
        damping,
        jnp.transpose(jacobians, (2, 3, 0, 1)),
        jnp.transpose(giles_real, (2, 3, 0, 1)),
        jnp.transpose(giles_imag, (2, 3, 0, 1)),
        blades,
        jnp.transpose(mode_orders, (0, 2, 1)),
        cell_map,
    )


def solution(mesh):
    rows, pitches = mesh.shape["row"], mesh.shape["pitch"]

    def step(*args):
        return on_device(rows, pitches, *args)

    placed = (
        P(None, "row", "span", "pitch"),
        P(None, "row", "span", "pitch"),
        P(None, "row", "span", "pitch"),
        P("row", "span", "pitch"),
        P("row", None, None, None),
        P(),
        P(),
        P(),
        P(),
        P("row", None),
    )
    return jax.shard_map(
        step,
        mesh=mesh,
        in_specs=placed,
        out_specs=P(None, "row", "span", "pitch"),
        check_vma=False,
    )
```
